128 devices in a mesh: req: 8 (over x, core), exp: 16 (over y, z).
Axes of the slice: x: 4, y: 4, z: 4, core: 2. Of those that a mesh axis runs over, the one named last changes fastest.
Arguments:
- tokens: bfloat16 [16384, 2048], P(('req', 'exp')), may hold values from -6 to 6
- norm_gains: float32 [2, 2048], replicated, may hold values from 0.25 to 1.75
- w_query: bfloat16 [2048, 4, 2048], P(None, None, 'exp'), may hold values from -0.125 to 0.125
- w_keyval: bfloat16 [2048, 2, 2048], P(None, None, 'exp'), may hold values from -0.125 to 0.125
- w_out: bfloat16 [4, 2048, 2048], P(None, 'exp'), may hold values from -0.125 to 0.125
- page_pool: bfloat16 [32, 128, 16, 256], P('req', None, 'exp'), may hold values from -3000 to 3000
- page_dest: int32 [32], replicated, may hold values from 0 to 31, as said below
- prompt_lens: int32 [8, 4], P('req'), may hold values from 1 to 1024, 2048 in all within a row
- att_ids: int32 [16384, 2], P('req'), may hold values from 0 to 3, all different within a row
- att_gates: float32 [16384, 2], P('req'), may hold values from 0.1 to 1
- w_in: bfloat16 [2048, 2, 22528], P(None, None, 'exp'), may hold values from -0.125 to 0.125
- w_down: bfloat16 [22528, 2048], P('exp'), may hold values from -0.109375 to 0.109375
- moe_ids: int32 [16384, 2], P(('req', 'exp')), may hold values from 0 to 7, all different within a row; in each aligned block of 128 rows (0 to 127, 128 to 255, ...) at most 40 rows name the same one
- moe_gates: float32 [16384, 2], P(('req', 'exp')), may hold values from 0.1 to 1
- adapters: bfloat16 [64, 2, 16, 2048], P('exp'), may hold values from -0.25 to 0.25
- req_adapter: int32 [32], replicated, may hold values from 0 to 63, as said below
Outputs:
- layer_out: bfloat16 [16384, 2048], P(('req', 'exp'))
The draws below stay inside these ranges and needn't reach their ends.
Inputs may be any that keep to these rules, and one draw needn't show every extreme that they name: `page_dest`: pool slot g * 4 + p holds the pages of request ((g + s_p) mod the number of groups) * 4 + p, where the 4 shifts s_p are distinct: a group's slots go to 4 different groups, and each group receives one request a slot. `prompt_lens`: the 4 lengths of a group sum to 2048. `att_ids`: the two ids of a token differ. `moe_ids`: the two ids of a token differ; among the 128 tokens of one device no expert is named by more than 40, a bound that some block reaches. `req_adapter`: exactly 16 distinct adapters are named, adapters 0 and 63 among them.
All inputs are finite; a program needn't handle non-finite values.
Results may differ from the reference program's by a relative error of at most 0.015.
Values may be sent and summed in bfloat16 or wider, within the bound.
A program may use at most 192 MiB of HBM per device.

```python
import math
import jax
import jax.numpy as jnp
import numpy as np
from jax import lax

D = 2048
HEADS = 16
HD = 128
AEXP = 4
EXPERTS = 8
FF = 2816
RANK = 16
USED = 16
RG = 4
CACHE = 128
TOK_DEV = 128
TOK_G = 2048
TOKENS = 16384
NREQ = 32
ADAPTERS = 64
CAP = 40
LMAX = 1024
N_REQ = 8
DEVICES = 128


def draw_page_pool(key, part):
    base = jnp.clip(jax.random.normal(key, (NREQ, CACHE, HEADS, 2 * HD), jnp.float32), -6.0, 6.0)
    return base.astype(jnp.bfloat16)


def draw_page_dest(key, part):
    group_total = NREQ // RG
    shifts = jax.random.permutation(key, group_total)[:RG]
    slot_index = jnp.arange(NREQ)
    owner = slot_index // RG
    within = slot_index % RG
    return ((owner + shifts[within]) % group_total * RG + within).astype(jnp.int32)


def draw_req_adapter(key, part):
    first_key = jax.random.fold_in(key, 11)
    second_key = jax.random.fold_in(key, 12)
    third_key = jax.random.fold_in(key, 13)
    middle_ids = 1 + jax.random.permutation(first_key, ADAPTERS - 2)[:USED - 2]
    ends = jnp.array([0, ADAPTERS - 1], dtype=jnp.int32)
    used_ids = jnp.concatenate([ends, middle_ids.astype(jnp.int32)])
    extra = jax.random.randint(second_key, (NREQ,), 0, USED)
    counter = jnp.arange(NREQ)
    basis = jnp.where(counter < USED, counter, extra)
    shuffle = jax.random.permutation(third_key, NREQ)
    return used_ids[basis[shuffle]].astype(jnp.int32)


def levels(stream_key, shape, pieces, low, largest):
    factor_of, own = 1.0, jax.random.fold_in(stream_key, 6)
    for dim, blocks in pieces:
        steps = jnp.exp(jax.random.uniform(jax.random.fold_in(own, dim), (blocks,), jnp.float32, low / len(pieces), largest / len(pieces)))
        factor_of = factor_of * jnp.repeat(steps, shape[dim] // blocks).reshape([-1 if axis == dim else 1 for axis in range(len(shape))])
    return factor_of


def choose_distinct(stream_key, rows, number_of, top, lift):
    order = jax.random.permutation(jax.random.fold_in(stream_key, 1), number_of)
    boost = order
    for power in range(3):
        boost = boost * boost // number_of
    boost = boost * lift // number_of
    tickets = jax.random.randint(jax.random.fold_in(stream_key, 2), (rows, number_of), 0, 4096) + boost
    holders = jax.random.permutation(jax.random.fold_in(stream_key, 3), rows)[jnp.arange(number_of) % rows]
    tickets = jnp.where(jnp.arange(rows)[:, None] == holders[None, :], 1 << 14, tickets)
    score = tickets * number_of + jnp.arange(number_of)
    return lax.top_k(score.astype(jnp.int32), top)[1].astype(jnp.int32)


def length_profile(number_of, total, bound, lean):
    weights = [(1 << 20) // math.isqrt(grade ** lean) + 1 for grade in range(2, number_of + 1)]
    spare, holding = total - bound - (number_of - 1), [1] * (number_of - 1)
    while spare > 0:
        candidates = [i for i in range(number_of - 1) if holding[i] < bound]
        mass, remaining = sum([weights[i] for i in candidates]), spare
        for i in candidates:
            more = min(bound - holding[i], max(1, remaining * weights[i] // mass), spare)
            holding[i] = holding[i] + more
            spare = spare - more
    return np.array([bound] + holding)


def uneven_parts(rng, count, total, bound, skew):
    if count == 2:
        one = jax.random.randint(rng, (), max(1, total - bound), min(bound, total - 1) + 1)
        return jnp.stack([one, total - one])
    tallies = jnp.asarray(length_profile(count, total, bound, skew), jnp.int32)
    twos = (count - 1) // 2
    giver, taker = tallies[1:1 + 2 * twos:2], tallies[2:2 + 2 * twos:2]
    margin = jnp.minimum(giver - 1, bound - taker)
    shifted = jax.random.randint(jax.random.fold_in(rng, 1), (twos,), 0, 1 << 20) % (margin + 1)
    tallies = tallies.at[1:1 + 2 * twos:2].set(giver - shifted).at[2:2 + 2 * twos:2].set(taker + shifted)
    return tallies[jax.random.permutation(jax.random.fold_in(rng, 2), count)]


def deal_out(rng, own, number, rows, amount, top, bound, slope):
    sequence = jax.random.permutation(rng, amount)
    heavy_load, ordinary = portions_of(amount, rows * top, bound, slope, True), portions_of(amount, rows * top, bound, slope, False)
    places = jnp.arange(amount)

    def named(tallies, turn):
        used = int((tallies > 0).sum())
        fixed = max(1, used // 4)
        passed = fixed + (places - fixed + turn * (used - fixed)) % max(1, amount - fixed)
        return jnp.zeros((amount,), jnp.int32).at[sequence[jnp.where(places < fixed, places, passed)]].set(jnp.asarray(tallies, jnp.int32))

    tallies = jnp.where(number % 4 == 0, named(heavy_load, number // 4), named(ordinary, number - number // 4 - 1))
    mixed = jax.random.permutation(jax.random.fold_in(own, 3), amount)
    source_of, taker = mixed[0:amount // 2 * 2:2], mixed[1:amount // 2 * 2:2]
    slack = jnp.minimum(tallies[source_of] - 1, bound - tallies[taker]) // 2
    slack = jnp.where((source_of == sequence[0]) | (taker == sequence[0]) | (tallies[taker] == 0), 0, jnp.maximum(slack, 0))
    passed = jax.random.randint(jax.random.fold_in(own, 4), (amount // 2,), 0, 1 << 20) % (slack + 1)
    tallies = tallies.at[source_of].add(-passed).at[taker].add(passed)
    items = jnp.searchsorted(jnp.cumsum(tallies), jnp.arange(rows * top), side="right").astype(jnp.int32)
    listing = items.reshape(top, rows).T
    listing = listing[jax.random.permutation(jax.random.fold_in(own, 1), rows)]
    turn = jax.random.randint(jax.random.fold_in(own, 2), (rows, 1), 0, top)
    return jnp.take_along_axis(listing, (jnp.arange(top)[None, :] + turn) % top, axis=1)


def portions_of(count, total, limit, lean, full):
    loads = [(1 << 20) // math.isqrt(grade ** lean) + 1 for grade in range(1, count + 1)]
    largest = limit if full else min(limit, max(-(-total // count), total * loads[0] // sum(loads)))
    least = 1 if total - largest >= count - 1 else 0
    counts, surplus = [largest] + [least] * (count - 1), total - largest - least * (count - 1)
    while surplus > 0:
        movable = [i for i in range(1, count) if counts[i] < largest] or [i for i in range(1, count) if counts[i] < limit]
        whole, budget = sum([loads[i] for i in movable]), surplus
        for i in movable:
            more = min(limit - counts[i], max(1, budget * loads[i] // whole), surplus)
            counts[i] = counts[i] + more
            surplus = surplus - more
    return np.array(counts)


def normal_values(stream_key, extent, deviation, reach, cuts=(), kind=jnp.bfloat16):
    level = levels(stream_key, extent, cuts, -0.22, 0.18) if cuts else 1.0
    values = jax.random.normal(stream_key, extent, jnp.float32) * deviation * level
    return jnp.minimum(jnp.maximum(values, -reach), reach).astype(kind)


def setup_inputs(seed: int = 0) -> dict:
    keys = jax.random.split(jax.random.key(seed), 17)
    tokens = normal_values(keys[0], (TOKENS, D), 1.0, 6.0, ((0, 128),))
    norm_gains = jnp.clip(1.0 + 0.15 * jax.random.normal(keys[1], (2, D), jnp.float32), 0.25, 1.75)
    w_query = normal_values(keys[2], (D, AEXP, HEADS * HD), D ** -0.5, 0.125, ((2, 16),))
    w_keyval = normal_values(keys[3], (D, 2, HEADS * HD), D ** -0.5, 0.125, ((2, 16),))
    w_out = normal_values(keys[4], (AEXP, HEADS * HD, D), (HEADS * HD) ** -0.5, 0.125, ((1, 16),))
    page_pool = draw_page_pool(jax.random.fold_in(keys[16], 71), 0)
    page_dest = draw_page_dest(jax.random.fold_in(keys[16], 71), 0)
    prompt_lens = jax.vmap(lambda own: uneven_parts(own, RG, TOK_G, LMAX, 2))(jax.random.split(keys[7], N_REQ)).reshape((N_REQ, RG)).astype(jnp.int32)
    att_ids = choose_distinct(keys[8], TOKENS, AEXP, 2, 0)
    att_gates = jnp.clip(0.1 + 0.9 * jax.random.uniform(keys[9], (TOKENS, 2), jnp.float32) ** levels(keys[9], (TOKENS, 2), ((0, 8),), -0.2, 0.2), 0.1, 1.0)
    w_in = normal_values(keys[10], (D, 2, EXPERTS * FF), D ** -0.5, 0.125, ((2, 16),))
    w_down = normal_values(keys[11], (EXPERTS * FF, D), FF ** -0.5, 0.109375, ((0, 16),))
    moe_ids_keys = jax.random.split(jax.random.fold_in(keys[12], 1), TOKENS // TOK_DEV)
    moe_ids_turns = jax.random.permutation(jax.random.fold_in(keys[12], 3), TOKENS // TOK_DEV)
    moe_ids = jax.vmap(lambda own, number: deal_out(jax.random.fold_in(keys[12], 2), own, number, TOK_DEV, EXPERTS, 2, CAP, 2))(moe_ids_keys, moe_ids_turns).reshape((TOKENS, 2))
    moe_gates = jnp.clip(0.1 + 0.9 * jax.random.uniform(keys[13], (TOKENS, 2), jnp.float32) ** levels(keys[13], (TOKENS, 2), ((0, 128),), -0.2, 0.2), 0.1, 1.0)
    adapters = normal_values(keys[14], (ADAPTERS, 2, RANK, D), (D // 4) ** -0.5, 0.25, ((0, 16),))
    req_adapter = draw_req_adapter(jax.random.fold_in(keys[16], 71), 0)
    return {"tokens": tokens, "norm_gains": norm_gains, "w_query": w_query, "w_keyval": w_keyval, "w_out": w_out, "page_pool": page_pool, "page_dest": page_dest, "prompt_lens": prompt_lens, "att_ids": att_ids, "att_gates": att_gates, "w_in": w_in, "w_down": w_down, "moe_ids": moe_ids, "moe_gates": moe_gates, "adapters": adapters, "req_adapter": req_adapter}


norm_eps = 1e-05

def rms_scale(values, gain):
    values = values.astype(jnp.float32)
    factor = lax.rsqrt(lax.optimization_barrier(jnp.mean(values * values, axis=-1, keepdims=True)) + norm_eps)
    return (values * factor * gain).astype(jnp.bfloat16)

def rotate(vectors, places):
    half_width = vectors.shape[-1] // 2
    steps_idx = jnp.arange(half_width, dtype=jnp.float32)
    inverse = jnp.power(10000.0, steps_idx * (-2.0 / vectors.shape[-1]))
    angles = places.astype(jnp.float32)[:, None] * inverse[None, :]
    angles = angles.reshape((places.shape[0],) + (1,) * (vectors.ndim - 2) + (half_width,))
    cosine = jnp.cos(angles)
    sine_part = jnp.sin(angles)
    former = vectors[..., :half_width]
    latter = vectors[..., half_width:]
    return jnp.concatenate([former * cosine - latter * sine_part, former * sine_part + latter * cosine], axis=-1)

def group_positions(lengths, total, cached):
    lengths = lengths.astype(jnp.int32)
    finish = jnp.cumsum(lengths).astype(jnp.int32)
    beginning = finish - lengths
    indices = jnp.arange(total, dtype=jnp.int32)
    segment = lax.optimization_barrier(jnp.sum((indices[:, None] >= finish[None, :]).astype(jnp.int32), axis=1)).astype(jnp.int32)
    member = segment[:, None] == jnp.arange(lengths.shape[0], dtype=jnp.int32)[None, :]
    offset = lax.optimization_barrier(jnp.sum(jnp.where(member, beginning[None, :], 0), axis=1)).astype(jnp.int32)
    return (segment, (cached + indices - offset).astype(jnp.int32))

def attend_head(queries, key_rows, val_rows, visible, scale_factor):
    scores = jnp.dot(queries, key_rows.T, preferred_element_type=jnp.float32) * scale_factor
    scores = jnp.where(visible, scores, -1e+30)
    highest = lax.optimization_barrier(jnp.max(scores, axis=-1, keepdims=True))
    raised = jnp.exp(scores - highest)
    weights = (raised / lax.optimization_barrier(jnp.sum(raised, axis=-1, keepdims=True))).astype(jnp.bfloat16)
    return jnp.dot(weights, val_rows, preferred_element_type=jnp.float32).astype(jnp.bfloat16)

def reference(tokens, norm_gains, w_query, w_keyval, w_out, page_pool, page_dest, prompt_lens, att_ids, att_gates, w_in, w_down, moe_ids, moe_gates, adapters, req_adapter):
    normed = rms_scale(tokens, norm_gains[0])
    segments, places = jax.vmap(lambda lengths: group_positions(lengths, TOK_G, CACHE))(prompt_lens)
    flat_places = places.reshape(TOKENS)
    queries = jnp.dot(normed, w_query.reshape(D, AEXP * HEADS * HD), preferred_element_type=jnp.float32)
    queries = rotate(queries.reshape(TOKENS, AEXP, HEADS, HD), flat_places).astype(jnp.bfloat16)
    chosen_rows = (jnp.arange(TOKENS, dtype=jnp.int32)[:, None] * AEXP + att_ids).reshape(-1).astype(jnp.int32)
    chosen = jnp.take(queries.reshape(TOKENS * AEXP, HEADS * HD), chosen_rows, axis=0)
    chosen = chosen.reshape(N_REQ, TOK_G * 2, HEADS, HD)
    keyval = jnp.dot(normed, w_keyval.reshape(D, 2 * HEADS * HD), preferred_element_type=jnp.float32)
    keyval = keyval.reshape(TOKENS, 2, HEADS, HD)
    new_keys = rotate(keyval[:, 0], flat_places).astype(jnp.bfloat16).reshape(N_REQ, TOK_G, HEADS, HD)
    new_values = keyval[:, 1].astype(jnp.bfloat16).reshape(N_REQ, TOK_G, HEADS, HD)
    arrived = jnp.zeros_like(page_pool).at[page_dest].set(page_pool)
    arrived = arrived.reshape(N_REQ, RG * CACHE, HEADS, 2 * HD)
    scale_factor = 1.0 / math.sqrt(HD)

    def group_attention(items):
        group_queries, group_keys, group_values, group_cache, group_segment = items
        key_rows = jnp.concatenate([group_cache[..., :HD], group_keys], axis=0)
        val_rows = jnp.concatenate([group_cache[..., HD:], group_values], axis=0)
        key_segment = jnp.concatenate([jnp.repeat(jnp.arange(RG, dtype=jnp.int32), CACHE), group_segment])
        key_index = jnp.concatenate([jnp.full((RG * CACHE,), -1, jnp.int32), jnp.arange(TOK_G, dtype=jnp.int32)])
        query_segment = jnp.repeat(group_segment, 2)
        query_index = jnp.repeat(jnp.arange(TOK_G, dtype=jnp.int32), 2)
        visible = (query_segment[:, None] == key_segment[None, :]) & (key_index[None, :] <= query_index[:, None])

        def head_step(triple):
            return attend_head(triple[0], triple[1], triple[2], visible, scale_factor)
        per_head = lax.map(head_step, (group_queries.transpose(1, 0, 2), key_rows.transpose(1, 0, 2), val_rows.transpose(1, 0, 2)))
        return per_head.transpose(1, 0, 2).reshape(TOK_G, 2, HEADS * HD)
    heads_out = lax.map(group_attention, (chosen, new_keys, new_values, arrived, segments))
    heads_out = heads_out.reshape(TOKENS, 2, HEADS * HD)
    slot_weights = jnp.where(att_ids[:, :, None] == jnp.arange(AEXP, dtype=jnp.int32)[None, None, :], att_gates[:, :, None], 0.0)
    mixed = jnp.einsum('tje,tjx->tex', slot_weights.astype(jnp.float32), heads_out.astype(jnp.float32), precision=lax.Precision.HIGHEST).astype(jnp.bfloat16)
    attended = jnp.dot(mixed.reshape(TOKENS, AEXP * HEADS * HD), w_out.reshape(AEXP * HEADS * HD, D), preferred_element_type=jnp.float32)
    hidden_state = (tokens.astype(jnp.float32) + attended).astype(jnp.bfloat16)
    hnorm = rms_scale(hidden_state, norm_gains[1])
    expert_out = jnp.zeros((TOKENS, D), jnp.float32)
    row_limit = DEVICES * CAP
    for expert in range(EXPERTS):
        routed = jnp.where(moe_ids == expert, moe_gates, 0.0)
        weight_row = lax.optimization_barrier(jnp.sum(routed, axis=1))
        is_taken = jnp.any(moe_ids == expert, axis=1)
        picked = jnp.nonzero(is_taken, size=row_limit, fill_value=0)[0]
        is_valid = jnp.arange(row_limit) < jnp.sum(is_taken.astype(jnp.int32))
        block_rows = jnp.take(hnorm, picked, axis=0)
        gate_part = jnp.dot(block_rows, w_in[:, 0, expert * FF:(expert + 1) * FF], preferred_element_type=jnp.float32)
        up_part = jnp.dot(block_rows, w_in[:, 1, expert * FF:(expert + 1) * FF], preferred_element_type=jnp.float32)
        inner_act = (jax.nn.silu(gate_part) * up_part).astype(jnp.bfloat16)
        result = jnp.dot(inner_act, w_down[expert * FF:(expert + 1) * FF], preferred_element_type=jnp.float32)
        factor_rows = jnp.where(is_valid, jnp.take(weight_row, picked), 0.0)
        expert_out = expert_out.at[picked].add(result * factor_rows[:, None])
    group_choice = req_adapter.reshape(N_REQ, RG)

    def group_adapter(items):
        group_rows, group_segment, chosen_ids = items
        factors = jnp.take(adapters, chosen_ids, axis=0)
        lowrank = jnp.einsum('td,qrd->tqr', group_rows.astype(jnp.float32), factors[:, 0].astype(jnp.float32))
        member = group_segment[:, None] == jnp.arange(RG, dtype=jnp.int32)[None, :]
        lowrank = jnp.where(member[:, :, None], lowrank, 0.0).astype(jnp.bfloat16)
        return jnp.einsum('tqr,qrd->td', lowrank.astype(jnp.float32), factors[:, 1].astype(jnp.float32))
    delta = lax.map(group_adapter, (hnorm.reshape(N_REQ, TOK_G, D), segments, group_choice)).reshape(TOKENS, D)
    return (hidden_state.astype(jnp.float32) + expert_out + delta).astype(jnp.bfloat16)
```

```python
import math

import jax
import jax.numpy as jnp
import numpy as np
from jax import lax
from jax.experimental import pallas as pl
from jax.experimental.pallas import tpu as pltpu
from jax.sharding import PartitionSpec as P

HD = 128
AEXP = 4
EXPERTS = 8
CACHE = 128
CAP = 40
SIDE = 4
MESH = pl.DeviceIdType.MESH
F32, BF16, I32 = jnp.float32, jnp.bfloat16, jnp.int32

norm_eps = 1e-05


def rms_scale(values, gain):
    values = values.astype(F32)
    factor = lax.rsqrt(jnp.mean(values * values, axis=-1, keepdims=True) + norm_eps)
    return (values * factor * gain).astype(BF16)


def place():
    me = lax.axis_index("exp")
    return me, lax.div(me, SIDE), lax.rem(me, SIDE)


def beside(y, z, axis, step):
    if axis == 0:
        return lax.rem(y + step, SIDE) * SIDE + z
    return y * SIDE + lax.rem(z + step, SIDE)


def shard_at(y, z, half, first, second):
    if half == 0:
        return lax.rem(y + first, SIDE) * SIDE + lax.rem(z + second, SIDE)
    return lax.rem(y + second, SIDE) * SIDE + lax.rem(z + first, SIDE)


def meet_neighbours(y, z):
    barrier = pltpu.get_barrier_semaphore()
    for axis in (0, 1):
        for step in (1, 3):
            pl.semaphore_signal(
                barrier, inc=1, device_id={"exp": beside(y, z, axis, step)}, device_id_type=MESH
            )
    return barrier


class Sender:
    def __init__(self, y, z, sems):
        self.y, self.z, self.sems, self.sent = y, z, sems, []

    def copy(self, src, dst, recv, axis, step, slot):
        return pltpu.make_async_remote_copy(
            src_ref=src,
            dst_ref=dst,
            send_sem=self.sems.at[slot],
            recv_sem=recv,
            device_id={"exp": beside(self.y, self.z, axis, step)},
            device_id_type=MESH,
        )

    def send(self, src, dst, recv, axis, step):
        done = self.copy(src, dst, recv, axis, step, len(self.sent))
        done.start()
        self.sent.append(done)

    def arrive(self, dst, recv):
        self.copy(dst, dst, recv, 0, 1, 0).wait_recv()

    def finish(self):
        for done in self.sent:
            done.wait_send()


def ends_of(lens):
    ends, total = [], 0
    for r in range(4):
        total = total + lens[r]
        ends.append(total)
    return ends


def start_of(rows, ends):
    begin = jnp.zeros_like(rows)
    for end in ends[:3]:
        begin = jnp.where(rows >= end, end, begin)
    return begin


def project_kernel(
    lens, tok, gain, wq, wkv, freq, ids, q_out, k_out, v_out, held, w, acc, idt, ssem, rsem
):
    me, y, z = place()
    barrier = meet_neighbours(y, z)
    held[me] = rms_scale(tok[...], gain[0:1]).reshape(4, 32, -1)
    pl.semaphore_wait(barrier, 4)
    link = Sender(y, z, ssem)

    def send(s, piece, axis, step):
        link.send(held.at[s, piece], held.at[s, piece], rsem.at[s, piece], axis, step)

    def arrive(s, half):
        for p in (0, 1):
            link.arrive(held.at[s, 2 * half + p], rsem.at[s, 2 * half + p])

    for second in (0, 1):
        for half in (0, 1):
            for p in (0, 1):
                for step in (1, 3):
                    send(me, 2 * half + p, (half + second) % 2, step)

    rows256 = lax.broadcasted_iota(I32, (256, 256), 0)
    cols256 = lax.broadcasted_iota(I32, (256, 256), 1)
    by4 = (cols256 == lax.rem(rows256, 64) * 4 + lax.div(rows256, 64)).astype(BF16)
    by2 = (cols256 == lax.rem(rows256, 128) * 2 + lax.div(rows256, 128)).astype(BF16)

    def split4(b, carry):
        part = jnp.dot(by4, wq[pl.ds(b * 256, 256), :], preferred_element_type=F32).astype(BF16)
        for e in range(4):
            w[pl.ds(b * 64, 64), e * HD : (e + 1) * HD] = part[e * 64 : (e + 1) * 64]
        return carry

    def split2(b, carry):
        part = jnp.dot(by2, wkv[pl.ds(b * 256, 256), :], preferred_element_type=F32).astype(BF16)
        for e in range(2):
            w[pl.ds(b * 128, 128), (4 + e) * HD : (5 + e) * HD] = part[e * 128 : (e + 1) * 128]
        return carry

    lax.fori_loop(0, 32, split4, 0)
    lax.fori_loop(0, 16, split2, 0)

    def turn_ids(b, carry):
        at = pl.ds(pl.multiple_of(b * 128, 128), 128)
        block = jnp.concatenate([ids[:, at], jnp.zeros((6, 128), I32)], axis=0)
        idt[at, :] = block.astype(F32).T
        return carry

    lax.fori_loop(0, 16, turn_ids, 0)
    ends = ends_of(lens)
    lane = lax.broadcasted_iota(I32, (256, HD), 1)

    def project(half, across):
        shards = [a * (4 - 3 * half) + across * (1 + 3 * half) for a in range(4)]
        lhs = jnp.concatenate(
            [held[s, pl.ds(2 * half, 2)].reshape(64, -1) for s in shards], axis=0
        )
        acc[...] = jnp.dot(lhs, w[...], preferred_element_type=F32)
        starts = [pl.multiple_of(s * 128 + half * 64, 64) for s in shards]
        rows = jnp.concatenate(
            [lax.broadcasted_iota(I32, (64, 1), 0) + at for at in starts], axis=0
        )
        places = CACHE + rows - start_of(rows, ends)
        angle = places.astype(F32) * freq[...]
        cosine = jnp.cos(angle)
        sine = jnp.sin(angle)
        sine = jnp.where(lane < HD // 2, -sine, sine)

        def turn(v):
            return (v * cosine + pltpu.roll(v, HD // 2, 1) * sine).astype(BF16)

        named = jnp.concatenate([idt[pl.ds(at, 64), :] for at in starts], axis=0)
        slots = []
        for j in (0, 1):
            pick = acc[:, 0:HD]
            for e in range(1, 4):
                pick = jnp.where(named[:, j : j + 1] == float(e), acc[:, e * HD : (e + 1) * HD], pick)
            slots.append(turn(pick))
        keys = turn(acc[:, 4 * HD : 5 * HD])
        values = acc[:, 5 * HD : 6 * HD].astype(BF16)
        for a in range(4):
            at, piece = pl.ds(starts[a], 64), slice(a * 64, (a + 1) * 64)
            q_out[at, 0:HD] = slots[0][piece]
            q_out[at, HD : 2 * HD] = slots[1][piece]
            k_out[at, :] = keys[piece]
            v_out[at, :] = values[piece]

    for half in (0, 1):
        for first, piece, step in ((3, 0, 1), (1, 1, 3)):
            s = shard_at(y, z, half, first, 0)
            arrive(s, half)
            send(s, 2 * half + piece, half, step)
            for p in (0, 1):
                for onward in (1, 3):
                    send(s, 2 * half + p, 1 - half, onward)
    for half in (0, 1):
        s = shard_at(y, z, half, 2, 0)
        arrive(s, half)
        for p in (0, 1):
            for onward in (1, 3):
                send(s, 2 * half + p, 1 - half, onward)

    def second_of(half):
        return z * (1 - half) + y * half

    def own_step(n, carry):
        project(n, second_of(n))
        return carry

    lax.fori_loop(0, 2, own_step, 0)
    for first in (0, 3, 1, 2):
        for half in (0, 1):
            for second, piece, step in ((3, 0, 1), (1, 1, 3)):
                s = shard_at(y, z, half, first, second)
                arrive(s, half)
                send(s, 2 * half + piece, 1 - half, step)

    def near_step(n, carry):
        half = lax.div(n, 2)
        project(half, lax.rem(second_of(half) + 1 + 2 * lax.rem(n, 2), SIDE))
        return carry

    lax.fori_loop(0, 4, near_step, 0)
    for half in (0, 1):
        for first in (0, 3, 1, 2):
            arrive(shard_at(y, z, half, first, 2), half)

    def far_step(n, carry):
        project(n, lax.rem(second_of(n) + 2, SIDE))
        return carry

    lax.fori_loop(0, 2, far_step, 0)
    link.finish()


def project(tokens, norm_gains, wq, wkv, lens, ids):
    rows = tokens.shape[0] * 16
    width = tokens.shape[1]
    lanes = np.arange(HD) % (HD // 2)
    freq = np.power(10000.0, lanes * (-2.0 / HD)).astype(np.float32)[None, :]
    vmem = pl.BlockSpec(memory_space=pltpu.VMEM)
    return pl.pallas_call(
        project_kernel,
        out_shape=(
            jax.ShapeDtypeStruct((rows, 2 * HD), BF16),
            jax.ShapeDtypeStruct((rows, HD), BF16),
            jax.ShapeDtypeStruct((rows, HD), BF16),
        ),
        in_specs=[pl.BlockSpec(memory_space=pltpu.SMEM)] + [vmem] * 6,
        out_specs=(vmem, vmem, vmem),
        scratch_shapes=[
            pltpu.VMEM((16, 4, 32, width), BF16),
            pltpu.VMEM((width, 6 * HD), BF16),
            pltpu.VMEM((256, 6 * HD), F32),
            pltpu.VMEM((rows, 8), F32),
            pltpu.SemaphoreType.DMA((60,)),
            pltpu.SemaphoreType.DMA((16, 4)),
        ],
        compiler_params=pltpu.CompilerParams(collective_id=0, has_side_effects=True),
        name="gather_project",
    )(lens, tokens, norm_gains, wq, wkv, jnp.asarray(freq), ids)


def attend_kernel(lens, sender, q, k, v, pages, ids, gates, out, acc):
    block = pl.program_id(0)
    ends = ends_of(lens)
    first = block * 128
    last = first + 127
    scale = 1.0 / math.sqrt(HD)
    queries = jnp.concatenate([q[:, 0:HD], q[:, HD : 2 * HD]], axis=0)
    rows = lax.broadcasted_iota(I32, (128, 1), 0) + first
    rows = jnp.concatenate([rows, rows], axis=0)
    begin = start_of(rows, ends)
    low, high, low_start = 0, 0, 0
    for end in ends[:3]:
        low = low + (first >= end).astype(I32)
        high = high + (last >= end).astype(I32)
        low_start = jnp.where(first >= end, end, low_start)
    acc[...] = jnp.zeros_like(acc)

    def fold(state, keys, values, visible):
        top, total = state
        scores = lax.dot_general(
            queries, keys, (((1,), (1,)), ((), ())), preferred_element_type=F32
        )
        scores = jnp.where(visible, scores * scale, -1e30)
        peak = jnp.maximum(top, jnp.max(scores, axis=-1, keepdims=True))
        kept = jnp.exp(top - peak)
        raised = jnp.exp(scores - peak)
        acc[...] = acc[...] * kept + jnp.dot(
            raised.astype(BF16), values, preferred_element_type=F32
        )
        return peak, total * kept + jnp.sum(raised, axis=-1, keepdims=True)

    def cached_step(r, state):
        begins = jnp.where(r == 0, 0, jnp.where(r == 1, ends[0], jnp.where(r == 2, ends[1], ends[2])))
        came = sender[r]
        page = pages[came]
        mine = jnp.broadcast_to(begin == begins, (256, CACHE))
        return fold(state, page[:, 0:HD], page[:, HD : 2 * HD], mine)

    def key_step(b, state):
        at = pl.ds(pl.multiple_of(b * 256, 256), 256)
        cols = lax.broadcasted_iota(I32, (256, 256), 1) + b * 256
        return fold(state, k[at, :], v[at, :], (cols >= begin) & (cols <= rows))

    state = (jnp.full((256, 1), -1e30, F32), jnp.zeros((256, 1), F32))
    state = lax.fori_loop(low, high + 1, cached_step, state)
    state = lax.fori_loop(lax.div(low_start, 256), lax.div(last, 256) + 1, key_step, state)
    heads = (acc[...] / state[1]).astype(BF16).astype(F32)
    named = jnp.concatenate([ids[...], jnp.zeros((6, 128), I32)], axis=0).astype(F32).T
    weight = jnp.concatenate([gates[...], jnp.zeros((6, 128), F32)], axis=0).T
    for e in range(AEXP):
        mixed = jnp.zeros((128, HD), F32)
        for j in (0, 1):
            part = heads[j * 128 : (j + 1) * 128] * weight[:, j : j + 1]
            mixed = mixed + jnp.where(named[:, j : j + 1] == float(e), part, 0.0)
        out[:, e * HD : (e + 1) * HD] = mixed.astype(BF16)


def attend(q, k, v, pages, lens, sender, ids, gates):
    rows = q.shape[0]
    smem = pl.BlockSpec(memory_space=pltpu.SMEM)
    return pl.pallas_call(
        attend_kernel,
        out_shape=jax.ShapeDtypeStruct((rows, AEXP * HD), BF16),
        grid=(rows // 128,),
        in_specs=[
            smem,
            smem,
            pl.BlockSpec((128, 2 * HD), lambda i: (i, 0)),
            pl.BlockSpec((rows, HD), lambda i: (0, 0)),
            pl.BlockSpec((rows, HD), lambda i: (0, 0)),
            pl.BlockSpec(pages.shape, lambda i: (0, 0, 0)),
            pl.BlockSpec((2, 128), lambda i: (0, i)),
            pl.BlockSpec((2, 128), lambda i: (0, i)),
        ],
        out_specs=pl.BlockSpec((128, AEXP * HD), lambda i: (i, 0)),
        scratch_shapes=[pltpu.VMEM((256, HD), F32)],
        name="attend_mix",
    )(lens, sender, q, k, v, pages, ids, gates)


ORDER = (2, 1, 3, 0)


def reduce_kernel(
    mixed, w, tok, gain, hidden, hnorm, far, near, own, rx_far, rx_near, far2, near2, rx_far2, rx_near2,
    ssem, far_sem, near_sem, far2_sem, near2_sem,
):
    me, y, z = place()
    barrier = meet_neighbours(y, z)
    link = Sender(y, z, ssem)

    def partial(half, first):
        one = lax.rem(y * (1 - half) + z * half + first, SIDE)
        parts = []
        for offset in ORDER:
            two = lax.rem(z * (1 - half) + y * half + offset, SIDE)
            s = one * (4 - 3 * half) + two * (1 + 3 * half)
            parts.append(mixed[pl.ds(pl.multiple_of(s * 128 + half * 64, 64), 64), :])
        return jnp.dot(jnp.concatenate(parts, axis=0), w[...], preferred_element_type=F32)

    def far_step(half, carry):
        far[half] = partial(half, 2).astype(BF16).reshape(far.shape[1:])
        return carry

    lax.fori_loop(0, 2, far_step, 0)
    pl.semaphore_wait(barrier, 4)
    for i in range(4):
        for half in (0, 1):
            for p in (0, 1):
                link.send(
                    far.at[half, i, p], rx_far.at[half, p, i], far_sem.at[half, p, i], half, 1 + 2 * p
                )

    def near_step(n, carry):
        half, way = lax.div(n, 2), lax.rem(n, 2)
        near[half, way] = partial(half, 1 + 2 * way).astype(BF16).reshape(near.shape[2:])
        return carry

    lax.fori_loop(0, 4, near_step, 0)

    def send_near(half, way, i, p):
        link.send(
            near.at[half, way, i, p],
            rx_near.at[half, way, i, p],
            near_sem.at[half, way, i, p],
            half,
            1 + 2 * way,
        )

    for i in range(4):
        for half in (0, 1):
            for way in (0, 1):
                send_near(half, way, i, 1 - way)

    def own_step(half, carry):
        own[half] = partial(half, 0).reshape(own.shape[1:])
        return carry

    lax.fori_loop(0, 2, own_step, 0)

    for i in range(4):
        for half in (0, 1):
            for way in (0, 1):
                link.arrive(rx_far.at[half, way, i], far_sem.at[half, way, i])
                near[half, way, i, way] = (
                    near[half, way, i, way].astype(F32) + rx_far[half, way, i].astype(F32)
                ).astype(BF16)
        for half in (0, 1):
            for way in (0, 1):
                send_near(half, way, i, way)

    def total(half, i):
        for way in (0, 1):
            for p in (0, 1):
                link.arrive(rx_near.at[half, way, i, p], near_sem.at[half, way, i, p])
        summed = own[half, i]
        for way in (0, 1):
            summed = summed + rx_near[half, way, i].astype(F32)
        return summed

    def send_near2(half, way, p):
        link.send(
            near2.at[half, way, p],
            rx_near2.at[half, way, p],
            near2_sem.at[half, way, p],
            1 - half,
            1 + 2 * way,
        )

    for half in (0, 1):
        far2[half] = total(half, 0).astype(BF16)
    for half in (0, 1):
        for p in (0, 1):
            link.send(far2.at[half, p], rx_far2.at[half, p], far2_sem.at[half, p], 1 - half, 1 + 2 * p)
    for way in (0, 1):
        for half in (0, 1):
            near2[half, way] = total(half, 1 + way).astype(BF16)
        for half in (0, 1):
            send_near2(half, way, 1 - way)
    for way in (0, 1):
        for half in (0, 1):
            link.arrive(rx_far2.at[half, way], far2_sem.at[half, way])
            near2[half, way, way] = (
                near2[half, way, way].astype(F32) + rx_far2[half, way].astype(F32)
            ).astype(BF16)
        for half in (0, 1):
            send_near2(half, way, way)
    for half in (0, 1):
        own[half, 3] = total(half, 3)
    for half in (0, 1):
        summed = own[half, 3]
        for way in (0, 1):
            for p in (0, 1):
                link.arrive(rx_near2.at[half, way, p], near2_sem.at[half, way, p])
            summed = summed + rx_near2[half, way].astype(F32)
        rows = slice(half * 64, (half + 1) * 64)
        state = (tok[rows, :].astype(F32) + summed.reshape(64, -1)).astype(BF16)
        hidden[rows, :] = state
        hnorm[rows, :] = rms_scale(state, gain[1:2])
    link.finish()


def reduce_out(mixed, w_out, tokens, norm_gains):
    width = tokens.shape[1]
    vmem = pl.BlockSpec(memory_space=pltpu.VMEM)
    shape = jax.ShapeDtypeStruct(tokens.shape, BF16)
    piece = (32, width)
    dma = pltpu.SemaphoreType.DMA
    return pl.pallas_call(
        reduce_kernel,
        out_shape=(shape, shape),
        in_specs=[vmem] * 4,
        out_specs=(vmem, vmem),
        scratch_shapes=[
            pltpu.VMEM((2, 4, 2) + piece, BF16),
            pltpu.VMEM((2, 2, 4, 2) + piece, BF16),
            pltpu.VMEM((2, 4, 2) + piece, F32),
            pltpu.VMEM((2, 2, 4) + piece, BF16),
            pltpu.VMEM((2, 2, 4, 2) + piece, BF16),
            pltpu.VMEM((2, 2) + piece, BF16),
            pltpu.VMEM((2, 2, 2) + piece, BF16),
            pltpu.VMEM((2, 2) + piece, BF16),
            pltpu.VMEM((2, 2, 2) + piece, BF16),
            dma((60,)),
            dma((2, 2, 4)),
            dma((2, 2, 4, 2)),
            dma((2, 2)),
            dma((2, 2, 2)),
        ],
        compiler_params=pltpu.CompilerParams(collective_id=1, has_side_effects=True),
        name="project_reduce",
    )(mixed, w_out, tokens, norm_gains)


def on_device(
    tokens,
    norm_gains,
    w_query,
    w_keyval,
    w_out,
    page_pool,
    page_dest,
    prompt_lens,
    att_ids,
    att_gates,
    w_in,
    w_down,
    moe_ids,
    moe_gates,
    adapters,
    req_adapter,
):
    groups = lax.axis_size("req")
    columns = lax.axis_size("exp")
    group_index = lax.axis_index("req")
    column_index = lax.axis_index("exp")
    tok_rows, width = tokens.shape
    slot_count = page_pool.shape[0]
    group_numbers = jnp.arange(groups, dtype=I32)
    lens = prompt_lens.reshape(-1)

    own_target = (
        lax.dynamic_slice_in_dim(page_dest, group_index * slot_count, slot_count) // slot_count
    )
    slot_for = jnp.sum(
        jnp.where(
            own_target[None, :] == group_numbers[:, None],
            jnp.arange(slot_count, dtype=I32)[None, :],
            0,
        ),
        axis=1,
    )
    outgoing = jnp.take(page_pool.reshape(slot_count, CACHE, 2 * HD), slot_for, axis=0)
    pages = lax.all_to_all(outgoing, "req", split_axis=0, concat_axis=0, tiled=True)
    pool_slots = jnp.arange(page_dest.shape[0], dtype=I32)
    wanted = group_index * slot_count + jnp.arange(slot_count, dtype=I32)
    sender = (
        jnp.sum(jnp.where(page_dest[None, :] == wanted[:, None], pool_slots[None, :], 0), axis=1)
        // slot_count
    )

    wanted_ids = lax.dynamic_slice_in_dim(req_adapter, group_index * slot_count, slot_count)
    local_ids = wanted_ids - column_index * adapters.shape[0]
    held_here = (local_ids >= 0) & (local_ids < adapters.shape[0])
    share = jnp.where(
        held_here[:, None, None, None],
        jnp.take(adapters, jnp.clip(local_ids, 0, adapters.shape[0] - 1), axis=0),
        jnp.zeros((), BF16),
    )
    share = share.reshape(columns, -1, width)
    pieces = lax.all_to_all(share, "exp", split_axis=0, concat_axis=0, tiled=True)
    whole = jnp.sum(pieces.astype(F32), axis=0).astype(BF16)
    spread = jnp.broadcast_to(whole[None], share.shape)
    group_factors = lax.all_to_all(spread, "exp", split_axis=0, concat_axis=0, tiled=True)
    group_factors = group_factors.reshape(slot_count, *adapters.shape[1:])

    ids = att_ids.T
    q, k, v = project(
        tokens,
        norm_gains,
        w_query.reshape(width * AEXP, HD),
        w_keyval.reshape(width * 2, HD),
        lens,
        ids,
    )
    mixed = attend(q, k, v, pages, lens, sender, ids, att_gates.T)
    hidden_state, hnorm = reduce_out(mixed, w_out.reshape(-1, width), tokens, norm_gains)

    expert_flat = moe_ids.reshape(-1)
    expert_hits = (expert_flat[:, None] == jnp.arange(EXPERTS, dtype=I32)[None, :]).astype(I32)
    earlier = jnp.cumsum(expert_hits, axis=0) - expert_hits
    route_slot = jnp.sum(earlier * expert_hits, axis=1) + expert_flat * CAP
    table_size = EXPERTS * CAP
    placing = (jnp.arange(table_size, dtype=I32)[:, None] == route_slot[None, :]).reshape(
        table_size, tok_rows, 2
    )
    placing = jnp.any(placing, axis=2).astype(BF16)
    packed = jnp.dot(placing, hnorm, preferred_element_type=F32).astype(BF16)
    packed = packed.reshape(EXPERTS, CAP, width)
    copies = columns // EXPERTS
    spread_rows = jnp.repeat(packed, copies, axis=0)
    arrived = lax.all_to_all(spread_rows, "exp", split_axis=0, concat_axis=0, tiled=True)
    flat_rows = arrived.reshape(-1, width)
    gate_up = jnp.einsum("nd,dkf->nkf", flat_rows, w_in, preferred_element_type=F32)
    inner_act = (jax.nn.silu(gate_up[:, 0]) * gate_up[:, 1]).astype(BF16)
    partial_out = jnp.dot(inner_act, w_down, preferred_element_type=F32).reshape(
        columns, CAP, width
    )
    returned = lax.all_to_all(
        partial_out.astype(BF16), "exp", split_axis=0, concat_axis=0, tiled=True
    ).astype(F32)
    summed = jnp.sum(returned.reshape(EXPERTS, copies, CAP, width), axis=1).reshape(
        table_size, width
    )
    routed_rows = jnp.take(summed, route_slot, axis=0).reshape(tok_rows, 2, width)
    expert_out = jnp.sum(routed_rows * moe_gates[:, :, None], axis=1)
    own_rows = column_index * tok_rows + jnp.arange(tok_rows, dtype=I32)
    own_segment = jnp.sum((own_rows[:, None] >= jnp.cumsum(lens)[None, :]).astype(I32), axis=1)
    lowrank = jnp.einsum("td,qrd->tqr", hnorm, group_factors[:, 0], preferred_element_type=F32)
    member = own_segment[:, None] == jnp.arange(slot_count, dtype=I32)[None, :]
    lowrank = jnp.where(member[:, :, None], lowrank, 0.0).astype(BF16)
    delta = jnp.einsum("tqr,qrd->td", lowrank, group_factors[:, 1], preferred_element_type=F32)
    return (hidden_state.astype(F32) + expert_out + delta).astype(BF16)


def solution(mesh):
    in_specs = (
        P(("req", "exp"), None),
        P(),
        P(None, None, "exp"),
        P(None, None, "exp"),
        P(None, "exp", None),
        P("req", None, "exp", None),
        P(),
        P("req", None),
        P("req", None),
        P("req", None),
        P(None, None, "exp"),
        P("exp", None),
        P(("req", "exp"), None),
        P(("req", "exp"), None),
        P("exp", None, None, None),
        P(),
    )
    out_specs = P(("req", "exp"), None)
    return jax.shard_map(
        on_device, mesh=mesh, in_specs=in_specs, out_specs=out_specs, check_vma=False
    )
```

```python
import math

import jax
import jax.numpy as jnp
import numpy as np
from jax import lax
from jax.experimental import pallas as pl
from jax.experimental.pallas import tpu as pltpu
from jax.sharding import PartitionSpec as P

HD = 128
AEXP = 4
EXPERTS = 8
CACHE = 128
CAP = 40
SIDE = 4
MESH = pl.DeviceIdType.MESH
F32, BF16, I32 = jnp.float32, jnp.bfloat16, jnp.int32

norm_eps = 1e-05


def rms_scale(values, gain):
    values = values.astype(F32)
    factor = lax.rsqrt(jnp.mean(values * values, axis=-1, keepdims=True) + norm_eps)
    return (values * factor * gain).astype(BF16)


def place():
    me = lax.axis_index("exp")
    return me, lax.div(me, SIDE), lax.rem(me, SIDE)


def beside(y, z, axis, step):
    if axis == 0:
        return lax.rem(y + step, SIDE) * SIDE + z
    return y * SIDE + lax.rem(z + step, SIDE)


def shard_at(y, z, half, first, second):
    if half == 0:
        return lax.rem(y + first, SIDE) * SIDE + lax.rem(z + second, SIDE)
    return lax.rem(y + second, SIDE) * SIDE + lax.rem(z + first, SIDE)


def meet_neighbours(y, z):
    barrier = pltpu.get_barrier_semaphore()
    for axis in (0, 1):
        for step in (1, 3):
            pl.semaphore_signal(
                barrier, inc=1, device_id={"exp": beside(y, z, axis, step)}, device_id_type=MESH
            )
    return barrier


def meet_all(axis, here, count):
    barrier = pltpu.get_barrier_semaphore()
    for step in range(1, count):
        other = lax.rem(here + step, count)
        pl.semaphore_signal(barrier, inc=1, device_id={axis: other}, device_id_type=MESH)
    return barrier


def to_peer(axis, other, src, dst, send_sem, recv_sem):
    return pltpu.make_async_remote_copy(
        src_ref=src,
        dst_ref=dst,
        send_sem=send_sem,
        recv_sem=recv_sem,
        device_id={axis: other},
        device_id_type=MESH,
    )


class Sender:
    def __init__(self, y, z, sems):
        self.y, self.z, self.sems, self.sent = y, z, sems, []

    def copy(self, src, dst, recv, axis, step, slot):
        return pltpu.make_async_remote_copy(
            src_ref=src,
            dst_ref=dst,
            send_sem=self.sems.at[slot],
            recv_sem=recv,
            device_id={"exp": beside(self.y, self.z, axis, step)},
            device_id_type=MESH,
        )

    def send(self, src, dst, recv, axis, step):
        done = self.copy(src, dst, recv, axis, step, len(self.sent))
        done.start()
        self.sent.append(done)

    def arrive(self, dst, recv):
        self.copy(dst, dst, recv, 0, 1, 0).wait_recv()

    def finish(self):
        for done in self.sent:
            done.wait_send()


def ends_of(lens):
    ends, total = [], 0
    for r in range(4):
        total = total + lens[r]
        ends.append(total)
    return ends


def start_of(rows, ends):
    begin = jnp.zeros_like(rows)
    for end in ends[:3]:
        begin = jnp.where(rows >= end, end, begin)
    return begin


def project_kernel(
    lens, dest, wanted, tok, gain, wq, wkv, freq, ids, pool, adapters,
    q_out, k_out, v_out, pages, factors,
    held, w, acc, idt, leaving, parts_out, parts_in, ssem, rsem, page_ssem, page_sem, part_ssem, part_sem,
):
    me, y, z = place()
    group = lax.axis_index("req")
    meet_all("exp", me, 16)
    barrier = meet_all("req", group, 8)
    held[me] = rms_scale(tok[...], gain[0:1]).reshape(4, 32, -1)
    pl.semaphore_wait(barrier, 22)
    link = Sender(y, z, ssem)

    def send(s, piece, axis, step):
        link.send(held.at[s, piece], held.at[s, piece], rsem.at[s, piece], axis, step)

    def arrive(s, half):
        for p in (0, 1):
            link.arrive(held.at[s, 2 * half + p], rsem.at[s, 2 * half + p])

    for second in (0, 1):
        for half in (0, 1):
            for p in (0, 1):
                for step in (1, 3):
                    send(me, 2 * half + p, (half + second) % 2, step)

    def page_for(other):
        block = pool[0]
        for p in range(1, 4):
            target = dest[group * 4 + p]
            block = jnp.where((target >= other * 4) & (target < other * 4 + 4), pool[p], block)
        return block

    def part_for(other):
        named = wanted[group * 4 + lax.div(other, 4)]
        block = jnp.zeros(parts_in.shape[1:], BF16)
        for a in range(4):
            block = jnp.where(named == me * 4 + a, adapters[a, lax.rem(other, 4)], block)
        return block

    def page_step(step, carry):
        other = lax.rem(group + step, 8)
        leaving[step] = page_for(other)
        return carry

    def part_step(step, carry):
        other = lax.rem(me + step, 16)
        parts_out[step] = part_for(other)
        return carry

    lax.fori_loop(1, 8, page_step, 0)
    lax.fori_loop(1, 16, part_step, 0)
    pages[group] = page_for(group)
    parts_in[0] = part_for(me)
    others = []
    for step in range(1, 8):
        others.append(
            to_peer(
                "req", lax.rem(group + step, 8), leaving.at[step], pages.at[group],
                page_ssem.at[step], page_sem.at[step],
            )
        )
    for step in range(1, 16):
        others.append(
            to_peer(
                "exp", lax.rem(me + step, 16), parts_out.at[step], parts_in.at[step],
                part_ssem.at[step], part_sem.at[step],
            )
        )
    for copy in others:
        copy.start()

    rows256 = lax.broadcasted_iota(I32, (256, 256), 0)
    cols256 = lax.broadcasted_iota(I32, (256, 256), 1)
    by4 = (cols256 == lax.rem(rows256, 64) * 4 + lax.div(rows256, 64)).astype(BF16)
    by2 = (cols256 == lax.rem(rows256, 128) * 2 + lax.div(rows256, 128)).astype(BF16)

    def split4(b, carry):
        part = jnp.dot(by4, wq[pl.ds(b * 256, 256), :], preferred_element_type=F32).astype(BF16)
        for e in range(4):
            w[pl.ds(b * 64, 64), e * HD : (e + 1) * HD] = part[e * 64 : (e + 1) * 64]
        return carry

    def split2(b, carry):
        part = jnp.dot(by2, wkv[pl.ds(b * 256, 256), :], preferred_element_type=F32).astype(BF16)
        for e in range(2):
            w[pl.ds(b * 128, 128), (4 + e) * HD : (5 + e) * HD] = part[e * 128 : (e + 1) * 128]
        return carry

    lax.fori_loop(0, 32, split4, 0)
    lax.fori_loop(0, 16, split2, 0)

    def turn_ids(b, carry):
        at = pl.ds(pl.multiple_of(b * 128, 128), 128)
        block = jnp.concatenate([ids[:, at], jnp.zeros((6, 128), I32)], axis=0)
        idt[at, :] = block.astype(F32).T
        return carry

    lax.fori_loop(0, 16, turn_ids, 0)
    ends = ends_of(lens)
    lane = lax.broadcasted_iota(I32, (256, HD), 1)

    def project(half, across):
        shards = [a * (4 - 3 * half) + across * (1 + 3 * half) for a in range(4)]
        lhs = jnp.concatenate(
            [held[s, pl.ds(2 * half, 2)].reshape(64, -1) for s in shards], axis=0
        )
        acc[...] = jnp.dot(lhs, w[...], preferred_element_type=F32)
        starts = [pl.multiple_of(s * 128 + half * 64, 64) for s in shards]
        rows = jnp.concatenate(
            [lax.broadcasted_iota(I32, (64, 1), 0) + at for at in starts], axis=0
        )
        places = CACHE + rows - start_of(rows, ends)
        angle = places.astype(F32) * freq[...]
        cosine = jnp.cos(angle)
        sine = jnp.sin(angle)
        sine = jnp.where(lane < HD // 2, -sine, sine)

        def turn(v):
            return (v * cosine + pltpu.roll(v, HD // 2, 1) * sine).astype(BF16)

        named = jnp.concatenate([idt[pl.ds(at, 64), :] for at in starts], axis=0)
        slots = []
        for j in (0, 1):
            pick = acc[:, 0:HD]
            for e in range(1, 4):
                pick = jnp.where(named[:, j : j + 1] == float(e), acc[:, e * HD : (e + 1) * HD], pick)
            slots.append(turn(pick))
        keys = turn(acc[:, 4 * HD : 5 * HD])
        values = acc[:, 5 * HD : 6 * HD].astype(BF16)
        for a in range(4):
            at, piece = pl.ds(starts[a], 64), slice(a * 64, (a + 1) * 64)
            q_out[at, 0:HD] = slots[0][piece]
            q_out[at, HD : 2 * HD] = slots[1][piece]
            k_out[at, :] = keys[piece]
            v_out[at, :] = values[piece]

    for half in (0, 1):
        for first, piece, step in ((3, 0, 1), (1, 1, 3)):
            s = shard_at(y, z, half, first, 0)
            arrive(s, half)
            send(s, 2 * half + piece, half, step)
            for p in (0, 1):
                for onward in (1, 3):
                    send(s, 2 * half + p, 1 - half, onward)
    for half in (0, 1):
        s = shard_at(y, z, half, 2, 0)
        arrive(s, half)
        for p in (0, 1):
            for onward in (1, 3):
                send(s, 2 * half + p, 1 - half, onward)

    def second_of(half):
        return z * (1 - half) + y * half

    def own_step(n, carry):
        project(n, second_of(n))
        return carry

    lax.fori_loop(0, 2, own_step, 0)
    for first in (0, 3, 1, 2):
        for half in (0, 1):
            for second, piece, step in ((3, 0, 1), (1, 1, 3)):
                s = shard_at(y, z, half, first, second)
                arrive(s, half)
                send(s, 2 * half + piece, 1 - half, step)

    def near_step(n, carry):
        half = lax.div(n, 2)
        project(half, lax.rem(second_of(half) + 1 + 2 * lax.rem(n, 2), SIDE))
        return carry

    lax.fori_loop(0, 4, near_step, 0)
    for half in (0, 1):
        for first in (0, 3, 1, 2):
            arrive(shard_at(y, z, half, first, 2), half)

    def far_step(n, carry):
        project(n, lax.rem(second_of(n) + 2, SIDE))
        return carry

    lax.fori_loop(0, 2, far_step, 0)
    for copy in others:
        copy.wait()
    total = parts_in[0].astype(F32)
    for step in range(1, 16):
        total = total + parts_in[step].astype(F32)
    factors[...] = total.astype(BF16)
    link.finish()


def project(tokens, norm_gains, wq, wkv, lens, ids, dest, wanted, pool, adapters):
    rows = tokens.shape[0] * 16
    width = tokens.shape[1]
    lanes = np.arange(HD) % (HD // 2)
    freq = np.power(10000.0, lanes * (-2.0 / HD)).astype(np.float32)[None, :]
    vmem = pl.BlockSpec(memory_space=pltpu.VMEM)
    return pl.pallas_call(
        project_kernel,
        out_shape=(
            jax.ShapeDtypeStruct((rows, 2 * HD), BF16),
            jax.ShapeDtypeStruct((rows, HD), BF16),
            jax.ShapeDtypeStruct((rows, HD), BF16),
            jax.ShapeDtypeStruct((8,) + pool.shape[1:], BF16),
            jax.ShapeDtypeStruct((8, width), BF16),
        ),
        in_specs=[pl.BlockSpec(memory_space=pltpu.SMEM)] * 3 + [vmem] * 8,
        out_specs=(vmem,) * 5,
        scratch_shapes=[
            pltpu.VMEM((16, 4, 32, width), BF16),
            pltpu.VMEM((width, 6 * HD), BF16),
            pltpu.VMEM((256, 6 * HD), F32),
            pltpu.VMEM((rows, 8), F32),
            pltpu.VMEM((8,) + pool.shape[1:], BF16),
            pltpu.VMEM((16, 8, width), BF16),
            pltpu.VMEM((16, 8, width), BF16),
            pltpu.SemaphoreType.DMA((60,)),
            pltpu.SemaphoreType.DMA((16, 4)),
            pltpu.SemaphoreType.DMA((8,)),
            pltpu.SemaphoreType.DMA((8,)),
            pltpu.SemaphoreType.DMA((16,)),
            pltpu.SemaphoreType.DMA((16,)),
        ],
        compiler_params=pltpu.CompilerParams(collective_id=0, has_side_effects=True),
        name="gather_project",
    )(lens, dest, wanted, tokens, norm_gains, wq, wkv, jnp.asarray(freq), ids, pool, adapters)


def attend_kernel(lens, dest, group, q, k, v, pages, ids, gates, out, acc):
    ends = ends_of(lens)
    rate = math.log2(math.e) / math.sqrt(HD)
    lane = lax.rem(lax.broadcasted_iota(I32, (1, 256), 1), 128)

    def block_step(block, carry):
        first = block * 128
        last = first + 127
        here = pl.ds(pl.multiple_of(first, 128), 128)
        queries = jnp.concatenate([q[here, 0:HD], q[here, HD : 2 * HD]], axis=0)
        rows = lane + first
        begin = start_of(rows, ends)
        low, high, low_start = 0, 0, 0
        for end in ends[:3]:
            low = low + (first >= end).astype(I32)
            high = high + (last >= end).astype(I32)
            low_start = jnp.where(first >= end, end, low_start)
        acc[...] = jnp.zeros_like(acc)

        def fold(state, keys, values, visible):
            top, total = state
            scores = lax.dot_general(
                keys, queries, (((1,), (1,)), ((), ())), preferred_element_type=F32
            )
            scores = jnp.where(visible, scores, -1e30)
            peak = jnp.maximum(top, jnp.max(scores, axis=0, keepdims=True))
            kept = jnp.exp2((top - peak) * rate)
            raised = jnp.exp2((scores - peak) * rate)
            acc[...] = acc[...] * kept + lax.dot_general(
                values, raised.astype(BF16), (((0,), (0,)), ((), ())), preferred_element_type=F32
            )
            return peak, total * kept + jnp.sum(raised, axis=0, keepdims=True)

        def cached_step(r, state):
            begins = jnp.where(
                r == 0, 0, jnp.where(r == 1, ends[0], jnp.where(r == 2, ends[1], ends[2]))
            )
            came = 0
            for g in range(8):
                came = came + g * (dest[g * 4 + r] == group[0] * 4 + r).astype(I32)
            page = pages[came]
            mine = jnp.broadcast_to(begin == begins, (CACHE, 256))
            return fold(state, page[:, 0:HD], page[:, HD : 2 * HD], mine)

        def key_step(b, state):
            at = pl.ds(pl.multiple_of(b * 256, 256), 256)
            cols = lax.broadcasted_iota(I32, (256, 256), 0) + b * 256
            return fold(state, k[at, :], v[at, :], (cols >= begin) & (cols <= rows))

        state = (jnp.full((1, 256), -1e30, F32), jnp.zeros((1, 256), F32))
        state = lax.fori_loop(low, high + 1, cached_step, state)
        state = lax.fori_loop(lax.div(low_start, 256), lax.div(last, 256) + 1, key_step, state)
        heads = (acc[...] / state[1]).astype(BF16).astype(F32)
        named = jnp.concatenate([ids[:, here], jnp.zeros((6, 128), I32)], axis=0).astype(F32).T
        weight = jnp.concatenate([gates[:, here], jnp.zeros((6, 128), F32)], axis=0).T
        parts = [heads[:, j * 128 : (j + 1) * 128].T * weight[:, j : j + 1] for j in (0, 1)]
        for e in range(AEXP):
            mixed = jnp.zeros((128, HD), F32)
            for j in (0, 1):
                mixed = mixed + jnp.where(named[:, j : j + 1] == float(e), parts[j], 0.0)
            out[here, e * HD : (e + 1) * HD] = mixed.astype(BF16)
        return carry

    lax.fori_loop(0, q.shape[0] // 128, block_step, 0)


def attend(q, k, v, pages, lens, dest, group, ids, gates):
    rows = q.shape[0]
    smem = pl.BlockSpec(memory_space=pltpu.SMEM)
    vmem = pl.BlockSpec(memory_space=pltpu.VMEM)
    return pl.pallas_call(
        attend_kernel,
        out_shape=jax.ShapeDtypeStruct((rows, AEXP * HD), BF16),
        in_specs=[smem] * 3 + [vmem] * 6,
        out_specs=vmem,
        scratch_shapes=[pltpu.VMEM((HD, 256), F32)],
        name="attend_mix",
    )(lens, dest, group, q, k, v, pages, ids, gates)


ORDER = (2, 1, 3, 0)


def reduce_kernel(
    mixed, w, tok, gain, hidden, hnorm, far, near, own, rx_far, rx_near, far2, near2, rx_far2, rx_near2,
    ssem, far_sem, near_sem, far2_sem, near2_sem,
):
    me, y, z = place()
    barrier = meet_neighbours(y, z)
    link = Sender(y, z, ssem)

    def partial(half, first):
        one = lax.rem(y * (1 - half) + z * half + first, SIDE)
        parts = []
        for offset in ORDER:
            two = lax.rem(z * (1 - half) + y * half + offset, SIDE)
            s = one * (4 - 3 * half) + two * (1 + 3 * half)
            parts.append(mixed[pl.ds(pl.multiple_of(s * 128 + half * 64, 64), 64), :])
        return jnp.dot(jnp.concatenate(parts, axis=0), w[...], preferred_element_type=F32)

    def far_step(half, carry):
        far[half] = partial(half, 2).astype(BF16).reshape(far.shape[1:])
        return carry

    lax.fori_loop(0, 2, far_step, 0)
    pl.semaphore_wait(barrier, 4)
    for i in range(4):
        for half in (0, 1):
            for p in (0, 1):
                link.send(
                    far.at[half, i, p], rx_far.at[half, p, i], far_sem.at[half, p, i], half, 1 + 2 * p
                )

    def near_step(n, carry):
        half, way = lax.div(n, 2), lax.rem(n, 2)
        near[half, way] = partial(half, 1 + 2 * way).astype(BF16).reshape(near.shape[2:])
        return carry

    lax.fori_loop(0, 4, near_step, 0)

    def send_near(half, way, i, p):
        link.send(
            near.at[half, way, i, p],
            rx_near.at[half, way, i, p],
            near_sem.at[half, way, i, p],
            half,
            1 + 2 * way,
        )

    for i in range(4):
        for half in (0, 1):
            for way in (0, 1):
                send_near(half, way, i, 1 - way)

    def own_step(half, carry):
        own[half] = partial(half, 0).reshape(own.shape[1:])
        return carry

    lax.fori_loop(0, 2, own_step, 0)

    for i in range(4):
        for half in (0, 1):
            for way in (0, 1):
                link.arrive(rx_far.at[half, way, i], far_sem.at[half, way, i])
                near[half, way, i, way] = (
                    near[half, way, i, way].astype(F32) + rx_far[half, way, i].astype(F32)
                ).astype(BF16)
        for half in (0, 1):
            for way in (0, 1):
                send_near(half, way, i, way)

    def total(half, i):
        for way in (0, 1):
            for p in (0, 1):
                link.arrive(rx_near.at[half, way, i, p], near_sem.at[half, way, i, p])
        summed = own[half, i]
        for way in (0, 1):
            summed = summed + rx_near[half, way, i].astype(F32)
        return summed

    def send_near2(half, way, p):
        link.send(
            near2.at[half, way, p],
            rx_near2.at[half, way, p],
            near2_sem.at[half, way, p],
            1 - half,
            1 + 2 * way,
        )

    for half in (0, 1):
        far2[half] = total(half, 0).astype(BF16)
    for half in (0, 1):
        for p in (0, 1):
            link.send(far2.at[half, p], rx_far2.at[half, p], far2_sem.at[half, p], 1 - half, 1 + 2 * p)
    for way in (0, 1):
        for half in (0, 1):
            near2[half, way] = total(half, 1 + way).astype(BF16)
        for half in (0, 1):
            send_near2(half, way, 1 - way)
    for way in (0, 1):
        for half in (0, 1):
            link.arrive(rx_far2.at[half, way], far2_sem.at[half, way])
            near2[half, way, way] = (
                near2[half, way, way].astype(F32) + rx_far2[half, way].astype(F32)
            ).astype(BF16)
        for half in (0, 1):
            send_near2(half, way, way)
    for half in (0, 1):
        own[half, 3] = total(half, 3)
    for half in (0, 1):
        summed = own[half, 3]
        for way in (0, 1):
            for p in (0, 1):
                link.arrive(rx_near2.at[half, way, p], near2_sem.at[half, way, p])
            summed = summed + rx_near2[half, way].astype(F32)
        rows = slice(half * 64, (half + 1) * 64)
        state = (tok[rows, :].astype(F32) + summed.reshape(64, -1)).astype(BF16)
        hidden[rows, :] = state
        hnorm[rows, :] = rms_scale(state, gain[1:2])
    link.finish()


def reduce_out(mixed, w_out, tokens, norm_gains):
    width = tokens.shape[1]
    vmem = pl.BlockSpec(memory_space=pltpu.VMEM)
    shape = jax.ShapeDtypeStruct(tokens.shape, BF16)
    piece = (32, width)
    dma = pltpu.SemaphoreType.DMA
    return pl.pallas_call(
        reduce_kernel,
        out_shape=(shape, shape),
        in_specs=[vmem] * 4,
        out_specs=(vmem, vmem),
        scratch_shapes=[
            pltpu.VMEM((2, 4, 2) + piece, BF16),
            pltpu.VMEM((2, 2, 4, 2) + piece, BF16),
            pltpu.VMEM((2, 4, 2) + piece, F32),
            pltpu.VMEM((2, 2, 4) + piece, BF16),
            pltpu.VMEM((2, 2, 4, 2) + piece, BF16),
            pltpu.VMEM((2, 2) + piece, BF16),
            pltpu.VMEM((2, 2, 2) + piece, BF16),
            pltpu.VMEM((2, 2) + piece, BF16),
            pltpu.VMEM((2, 2, 2) + piece, BF16),
            dma((60,)),
            dma((2, 2, 4)),
            dma((2, 2, 4, 2)),
            dma((2, 2)),
            dma((2, 2, 2)),
        ],
        compiler_params=pltpu.CompilerParams(collective_id=1, has_side_effects=True),
        name="project_reduce",
    )(mixed, w_out, tokens, norm_gains)


def expert_kernel(
    lens, hidden, hnorm, w_in, w_down, ids, gates, factors, out,
    packed, rx, back, ret, raw, w, wd, both, placed, table,
    wsem, dsem, ssem, rsem, bsem, esem, fsem, gsem,
):
    me = lax.axis_index("exp")
    width = hidden.shape[1]
    hidden_units = w_down.shape[0]
    barrier = meet_all("exp", me, 16)
    down = pltpu.make_async_copy(w_down, wd, dsem)
    down.start()

    def fetch(c):
        return pltpu.make_async_copy(
            w_in.at[pl.ds(c * 512, 512)], raw.at[lax.rem(c, 2)], wsem.at[lax.rem(c, 2)]
        )

    fetch(0).start()
    expert = lax.broadcasted_iota(I32, (8, 128), 0)
    hits = [ids[j : j + 1, :] == expert for j in (0, 1)]
    hit = (hits[0] | hits[1]).astype(F32)
    gate = jnp.where(hits[0], gates[0:1, :], 0.0) + jnp.where(hits[1], gates[1:2, :], 0.0)
    before = lax.broadcasted_iota(I32, (128, 128), 0) < lax.broadcasted_iota(I32, (128, 128), 1)
    rank = jnp.dot(hit.astype(BF16), before.astype(BF16), preferred_element_type=F32)
    slot = lax.broadcasted_iota(I32, (CAP, 128), 0).astype(F32)
    for e in range(EXPERTS):
        placed[e] = jnp.where((rank[e : e + 1] == slot) & (hit[e : e + 1] > 0.0), 1.0, 0.0)
    choice = placed[...].reshape(EXPERTS * CAP, 128).astype(BF16)
    packed[...] = (
        jnp.dot(choice, hnorm[...], preferred_element_type=F32).astype(BF16).reshape(packed.shape)
    )
    pl.semaphore_wait(barrier, 15)
    copies = []
    for step in range(1, 16):
        other = lax.rem(me + step, 16)
        copy = to_peer(
            "exp", other, packed.at[lax.div(other, 2)], rx.at[step], ssem.at[step], rsem.at[step]
        )
        copy.start()
        copies.append(copy)
    rx[0] = packed[lax.div(me, 2)]

    rows256 = lax.broadcasted_iota(I32, (256, 256), 0)
    cols256 = lax.broadcasted_iota(I32, (256, 256), 1)
    by2 = (cols256 == lax.rem(rows256, 128) * 2 + lax.div(rows256, 128)).astype(BF16)

    def split_step(c, carry):
        @pl.when(c + 1 < 8)
        def _():
            fetch(c + 1).start()

        fetch(c).wait()
        for b in (0, 1):
            part = jnp.dot(
                by2, raw[lax.rem(c, 2), b * 256 : (b + 1) * 256, :], preferred_element_type=F32
            ).astype(BF16)
            at = pl.ds(pl.multiple_of(c * 256 + b * 128, 128), 128)
            w[at, 0:hidden_units] = part[0:128]
            w[at, hidden_units : 2 * hidden_units] = part[128:256]
        return carry

    lax.fori_loop(0, 8, split_step, 0)
    down.wait()
    shares = []
    for part in (0, 1):
        for step in range(8 * part, 8 * part + 8):
            if step:
                copies[step - 1].wait_recv()
        if part == 1:
            for step in range(1, 16):
                copy = to_peer(
                    "exp", lax.rem(me + step, 16), factors, table.at[me], fsem.at[step], gsem.at[step]
                )
                copy.start()
                shares.append(copy)
        rows = rx[8 * part : 8 * part + 8].reshape(8 * CAP, width)
        both[...] = jnp.dot(rows, w[...], preferred_element_type=F32)
        gated = both[:, 0:hidden_units]
        inner = (gated / (1.0 + jnp.exp(-gated)) * both[:, hidden_units : 2 * hidden_units]).astype(BF16)
        back[8 * part : 8 * part + 8] = (
            jnp.dot(inner, wd[...], preferred_element_type=F32).astype(BF16).reshape(8, CAP, width)
        )
        for step in range(8 * part, 8 * part + 8):
            if step:
                copy = to_peer(
                    "exp", lax.rem(me + 16 - step, 16), back.at[step], ret.at[me],
                    bsem.at[step], esem.at[step],
                )
                copy.start()
                copies.append(copy)
            else:
                ret[me] = back[0]
    table[me] = factors[...]
    for copy in shares:
        copy.wait()
    rows = table[...].reshape(16 * 8, width)
    lowrank = lax.dot_general(
        hnorm[...], rows, (((1,), (1,)), ((), ())), preferred_element_type=F32
    )
    tokens = lax.broadcasted_iota(I32, (128, 1), 0) + me * 128
    ends = ends_of(lens)
    segment = jnp.zeros_like(tokens)
    for end in ends[:3]:
        segment = segment + (tokens >= end).astype(I32)
    lane = lax.broadcasted_iota(I32, (128, 128), 1)
    mine = (lax.div(lane, 32) == segment) & (lax.rem(lane, 32) < 16)
    lowrank = pltpu.roll(jnp.where(mine, lowrank, 0.0), 16, 1).astype(BF16)
    delta = jnp.dot(lowrank, rows, preferred_element_type=F32)
    total = hidden[...].astype(F32) + delta
    for step in range(1, 16):
        copies[14 + step].wait_recv()
    weight = jnp.concatenate(
        [placed[e // 2] * gate[e // 2 : e // 2 + 1] for e in range(16)], axis=0
    )
    high = weight.astype(BF16)
    low = (weight - high.astype(F32)).astype(BF16)
    came = ret[...].reshape(16 * CAP, width)
    for factor in (high, low):
        total = total + lax.dot_general(
            factor, came, (((0,), (0,)), ((), ())), preferred_element_type=F32
        )
    out[...] = total.astype(BF16)
    for copy in copies:
        copy.wait_send()


def experts(hidden, hnorm, w_in, w_down, ids, gates, factors, lens):
    rows, width = hidden.shape
    units = w_down.shape[0]
    smem = pl.BlockSpec(memory_space=pltpu.SMEM)
    vmem = pl.BlockSpec(memory_space=pltpu.VMEM)
    hbm = pl.BlockSpec(memory_space=pl.ANY)
    dma = pltpu.SemaphoreType.DMA
    return pl.pallas_call(
        expert_kernel,
        out_shape=jax.ShapeDtypeStruct((rows, width), BF16),
        in_specs=[smem, vmem, vmem, hbm, hbm, vmem, vmem, vmem],
        out_specs=vmem,
        scratch_shapes=[
            pltpu.VMEM((EXPERTS, CAP, width), BF16),
            pltpu.VMEM((16, CAP, width), BF16),
            pltpu.VMEM((16, CAP, width), BF16),
            pltpu.VMEM((16, CAP, width), BF16),
            pltpu.VMEM((2, 512, units), BF16),
            pltpu.VMEM((width, 2 * units), BF16),
            pltpu.VMEM((units, width), BF16),
            pltpu.VMEM((8 * CAP, 2 * units), F32),
            pltpu.VMEM((EXPERTS, CAP, 128), F32),
            pltpu.VMEM((16, 8, width), BF16),
            dma((2,)),
            dma,
            dma((16,)),
            dma((16,)),
            dma((16,)),
            dma((16,)),
            dma((16,)),
            dma((16,)),
        ],
        compiler_params=pltpu.CompilerParams(collective_id=2, has_side_effects=True),
        name="expert_exchange",
    )(lens, hidden, hnorm, w_in, w_down, ids, gates, factors)


def on_device(
    tokens,
    norm_gains,
    w_query,
    w_keyval,
    w_out,
    page_pool,
    page_dest,
    prompt_lens,
    att_ids,
    att_gates,
    w_in,
    w_down,
    moe_ids,
    moe_gates,
    adapters,
    req_adapter,
):
    width = tokens.shape[1]
    lens = prompt_lens.reshape(-1)
    group = lax.axis_index("req").reshape(1)
    ids = att_ids.T
    q, k, v, pages, factors = project(
        tokens,
        norm_gains,
        w_query.reshape(width * AEXP, HD),
        w_keyval.reshape(width * 2, HD),
        lens,
        ids,
        page_dest,
        req_adapter,
        page_pool.reshape(page_pool.shape[0], CACHE, 2 * HD),
        adapters.reshape(adapters.shape[0], 4, 8, width),
    )
    mixed = attend(q, k, v, pages, lens, page_dest, group, ids, att_gates.T)
    hidden, hnorm = reduce_out(mixed, w_out.reshape(-1, width), tokens, norm_gains)
    return experts(
        hidden,
        hnorm,
        w_in.reshape(width * 2, -1),
        w_down,
        moe_ids.T,
        moe_gates.T,
        factors,
        lens,
    )


def solution(mesh):
    in_specs = (
        P(("req", "exp"), None),
        P(),
        P(None, None, "exp"),
        P(None, None, "exp"),
        P(None, "exp", None),
        P("req", None, "exp", None),
        P(),
        P("req", None),
        P("req", None),
        P("req", None),
        P(None, None, "exp"),
        P("exp", None),
        P(("req", "exp"), None),
        P(("req", "exp"), None),
        P("exp", None, None, None),
        P(),
    )
    out_specs = P(("req", "exp"), None)
    return jax.shard_map(
        on_device, mesh=mesh, in_specs=in_specs, out_specs=out_specs, check_vma=False
    )
```

```python
import math

import jax
import jax.numpy as jnp
import numpy as np
from jax import lax
from jax.experimental import pallas as pl
from jax.experimental.pallas import tpu as pltpu
from jax.sharding import PartitionSpec as P

HD = 128
AEXP = 4
EXPERTS = 8
CACHE = 128
CAP = 40
SIDE = 4
RATE = math.log2(math.e) / math.sqrt(HD)
MESH = pl.DeviceIdType.MESH
F32, BF16, I32 = jnp.float32, jnp.bfloat16, jnp.int32

norm_eps = 1e-05


def rms_scale(values, gain):
    values = values.astype(F32)
    factor = lax.rsqrt(jnp.mean(values * values, axis=-1, keepdims=True) + norm_eps)
    return (values * factor * gain).astype(BF16)


def place():
    me = lax.axis_index("exp")
    return me, lax.div(me, SIDE), lax.rem(me, SIDE)


def beside(y, z, axis, step):
    if axis == 0:
        return lax.rem(y + step, SIDE) * SIDE + z
    return y * SIDE + lax.rem(z + step, SIDE)


def shard_at(y, z, half, first, second):
    if half == 0:
        return lax.rem(y + first, SIDE) * SIDE + lax.rem(z + second, SIDE)
    return lax.rem(y + second, SIDE) * SIDE + lax.rem(z + first, SIDE)


def meet_neighbours(y, z):
    barrier = pltpu.get_barrier_semaphore()
    for axis in (0, 1):
        for step in (1, 3):
            pl.semaphore_signal(
                barrier, inc=1, device_id={"exp": beside(y, z, axis, step)}, device_id_type=MESH
            )
    return barrier


def meet_all(axis, here, count):
    barrier = pltpu.get_barrier_semaphore()
    for step in range(1, count):
        other = lax.rem(here + step, count)
        pl.semaphore_signal(barrier, inc=1, device_id={axis: other}, device_id_type=MESH)
    return barrier


def to_peer(axis, other, src, dst, send_sem, recv_sem):
    return pltpu.make_async_remote_copy(
        src_ref=src,
        dst_ref=dst,
        send_sem=send_sem,
        recv_sem=recv_sem,
        device_id={axis: other},
        device_id_type=MESH,
    )


class Sender:
    def __init__(self, y, z, sems):
        self.y, self.z, self.sems, self.sent = y, z, sems, []

    def copy(self, src, dst, recv, axis, step, slot):
        return pltpu.make_async_remote_copy(
            src_ref=src,
            dst_ref=dst,
            send_sem=self.sems.at[slot],
            recv_sem=recv,
            device_id={"exp": beside(self.y, self.z, axis, step)},
            device_id_type=MESH,
        )

    def send(self, src, dst, recv, axis, step):
        done = self.copy(src, dst, recv, axis, step, len(self.sent))
        done.start()
        self.sent.append(done)

    def arrive(self, dst, recv):
        self.copy(dst, dst, recv, 0, 1, 0).wait_recv()

    def finish(self):
        for done in self.sent:
            done.wait_send()


def ends_of(lens):
    ends, total = [], 0
    for r in range(4):
        total = total + lens[r]
        ends.append(total)
    return ends


def start_of(rows, ends):
    begin = jnp.zeros_like(rows)
    for end in ends[:3]:
        begin = jnp.where(rows >= end, end, begin)
    return begin


def project_kernel(
    lens, dest, wanted, tok, gain, wq, wkv, freq, ids, gates, pool, adapters,
    q_out, k_out, v_out, pages, factors, idt,
    held, w, acc, waves, leaving, parts_out, parts_in, ssem, rsem, page_ssem, page_sem, part_ssem, part_sem,
):
    me, y, z = place()
    group = lax.axis_index("req")
    meet_all("exp", me, 16)
    barrier = meet_all("req", group, 8)
    held[me] = rms_scale(tok[...], gain[0:1]).reshape(4, 32, -1)
    pl.semaphore_wait(barrier, 22)
    link = Sender(y, z, ssem)

    def send(s, piece, axis, step):
        link.send(held.at[s, piece], held.at[s, piece], rsem.at[s, piece], axis, step)

    def arrive(s, half):
        for p in (0, 1):
            link.arrive(held.at[s, 2 * half + p], rsem.at[s, 2 * half + p])

    for second in (0, 1):
        for half in (0, 1):
            for p in (0, 1):
                for step in (1, 3):
                    send(me, 2 * half + p, (half + second) % 2, step)

    rows256 = lax.broadcasted_iota(I32, (256, 256), 0)
    cols256 = lax.broadcasted_iota(I32, (256, 256), 1)
    by4 = (cols256 == lax.rem(rows256, 64) * 4 + lax.div(rows256, 64)).astype(BF16)
    by2 = (cols256 == lax.rem(rows256, 128) * 2 + lax.div(rows256, 128)).astype(BF16)

    def split4(b, carry):
        part = jnp.dot(by4, wq[pl.ds(b * 256, 256), :], preferred_element_type=F32).astype(BF16)
        for e in range(4):
            w[pl.ds(b * 64, 64), e * HD : (e + 1) * HD] = part[e * 64 : (e + 1) * 64]
        return carry

    def split2(b, carry):
        part = jnp.dot(by2, wkv[pl.ds(b * 256, 256), :], preferred_element_type=F32).astype(BF16)
        for e in range(2):
            w[pl.ds(b * 128, 128), (4 + e) * HD : (5 + e) * HD] = part[e * 128 : (e + 1) * 128]
        return carry

    lax.fori_loop(0, 32, split4, 0, unroll=2)

    def turn_ids(b, carry):
        at = pl.ds(pl.multiple_of(b * 128, 128), 128)
        block = jnp.concatenate(
            [ids[:, at].astype(F32), gates[:, at], jnp.zeros((4, 128), F32)], axis=0
        )
        idt[at, :] = block.T
        rows = lax.broadcasted_iota(I32, (128, 1), 0) + b * 128
        places = CACHE + rows - start_of(rows, ends)
        waves[at, :] = jnp.cos(places.astype(F32) * freq[0:1] - freq[1:2])
        return carry

    ends = ends_of(lens)
    lane = lax.broadcasted_iota(I32, (256, HD), 1)

    def project(half, across):
        shards = [a * (4 - 3 * half) + across * (1 + 3 * half) for a in range(4)]
        lhs = jnp.concatenate(
            [held[s, pl.ds(2 * half, 2)].reshape(64, -1) for s in shards], axis=0
        )
        acc[...] = jnp.dot(lhs, w[...], preferred_element_type=F32)
        starts = [pl.multiple_of(s * 128 + half * 64, 64) for s in shards]
        wave = jnp.concatenate([waves[pl.ds(at, 64), :] for at in starts], axis=0)
        swapped = pltpu.roll(wave, HD // 2, 1)
        cosine = jnp.where(lane < HD // 2, wave, swapped)
        sine = jnp.where(lane < HD // 2, -swapped, wave)

        def turn(v):
            return (v * cosine + pltpu.roll(v, HD // 2, 1) * sine).astype(BF16)

        named = jnp.concatenate([idt[pl.ds(at, 64), :] for at in starts], axis=0)
        slots = []
        for j in (0, 1):
            pick = acc[:, 0:HD]
            for e in range(1, 4):
                pick = jnp.where(named[:, j : j + 1] == float(e), acc[:, e * HD : (e + 1) * HD], pick)
            slots.append(turn(pick * RATE))
        keys = turn(acc[:, 4 * HD : 5 * HD])
        values = acc[:, 5 * HD : 6 * HD].astype(BF16)
        for a in range(4):
            at, piece = pl.ds(starts[a], 64), slice(a * 64, (a + 1) * 64)
            q_out[at, 0:HD] = slots[0][piece]
            q_out[at, HD : 2 * HD] = slots[1][piece]
            k_out[at, :] = keys[piece]
            v_out[at, :] = values[piece]

    for half in (0, 1):
        for first, piece, step in ((3, 0, 1), (1, 1, 3)):
            s = shard_at(y, z, half, first, 0)
            arrive(s, half)
            send(s, 2 * half + piece, half, step)
            for p in (0, 1):
                for onward in (1, 3):
                    send(s, 2 * half + p, 1 - half, onward)
    lax.fori_loop(0, 16, split2, 0, unroll=2)
    lax.fori_loop(0, 16, turn_ids, 0)
    def page_for(other):
        block = pool[0]
        for p in range(1, 4):
            target = dest[group * 4 + p]
            block = jnp.where((target >= other * 4) & (target < other * 4 + 4), pool[p], block)
        return block

    def part_for(other):
        named = wanted[group * 4 + lax.div(other, 4)]
        block = jnp.zeros(parts_in.shape[1:], BF16)
        for a in range(4):
            block = jnp.where(named == me * 4 + a, adapters[a, lax.rem(other, 4)], block)
        return block

    def page_step(step, carry):
        other = lax.rem(group + step, 8)
        leaving[step] = page_for(other)
        return carry

    def part_step(step, carry):
        other = lax.rem(me + step, 16)
        parts_out[step] = part_for(other)
        return carry

    lax.fori_loop(1, 8, page_step, 0)
    lax.fori_loop(1, 16, part_step, 0)
    pages[group] = page_for(group)
    parts_in[0] = part_for(me)
    others = []
    for step in range(1, 8):
        others.append(
            to_peer(
                "req", lax.rem(group + step, 8), leaving.at[step], pages.at[group],
                page_ssem.at[step], page_sem.at[step],
            )
        )
    for step in range(1, 16):
        others.append(
            to_peer(
                "exp", lax.rem(me + step, 16), parts_out.at[step], parts_in.at[step],
                part_ssem.at[step], part_sem.at[step],
            )
        )
    for copy in others:
        copy.start()

    for half in (0, 1):
        s = shard_at(y, z, half, 2, 0)
        arrive(s, half)
        for p in (0, 1):
            for onward in (1, 3):
                send(s, 2 * half + p, 1 - half, onward)

    def second_of(half):
        return z * (1 - half) + y * half

    def own_step(n, carry):
        project(n, second_of(n))
        return carry

    lax.fori_loop(0, 2, own_step, 0)
    for first in (0, 3, 1, 2):
        for half in (0, 1):
            for second, piece, step in ((3, 0, 1), (1, 1, 3)):
                s = shard_at(y, z, half, first, second)
                arrive(s, half)
                send(s, 2 * half + piece, 1 - half, step)

    def near_step(n, carry):
        half = lax.div(n, 2)
        project(half, lax.rem(second_of(half) + 1 + 2 * lax.rem(n, 2), SIDE))
        return carry

    lax.fori_loop(0, 4, near_step, 0)
    for half in (0, 1):
        for first in (0, 3, 1, 2):
            arrive(shard_at(y, z, half, first, 2), half)

    def far_step(n, carry):
        project(n, lax.rem(second_of(n) + 2, SIDE))
        return carry

    lax.fori_loop(0, 2, far_step, 0)
    for copy in others:
        copy.wait()
    total = parts_in[0].astype(F32)
    for step in range(1, 16):
        total = total + parts_in[step].astype(F32)
    factors[...] = total.astype(BF16)
    link.finish()


def project(tokens, norm_gains, wq, wkv, lens, ids, gates, dest, wanted, pool, adapters):
    rows = tokens.shape[0] * 16
    width = tokens.shape[1]
    lanes = np.arange(HD) % (HD // 2)
    freq = np.stack(
        [np.power(10000.0, lanes * (-2.0 / HD)), (np.arange(HD) // (HD // 2)) * (np.pi / 2)]
    ).astype(np.float32)
    vmem = pl.BlockSpec(memory_space=pltpu.VMEM)
    return pl.pallas_call(
        project_kernel,
        out_shape=(
            jax.ShapeDtypeStruct((rows, 2 * HD), BF16),
            jax.ShapeDtypeStruct((rows, HD), BF16),
            jax.ShapeDtypeStruct((rows, HD), BF16),
            jax.ShapeDtypeStruct((8,) + pool.shape[1:], BF16),
            jax.ShapeDtypeStruct((8, width), BF16),
            jax.ShapeDtypeStruct((rows, 8), F32),
        ),
        in_specs=[pl.BlockSpec(memory_space=pltpu.SMEM)] * 3 + [vmem] * 9,
        out_specs=(vmem,) * 6,
        scratch_shapes=[
            pltpu.VMEM((16, 4, 32, width), BF16),
            pltpu.VMEM((width, 6 * HD), BF16),
            pltpu.VMEM((256, 6 * HD), F32),
            pltpu.VMEM((rows, HD), F32),
            pltpu.VMEM((8,) + pool.shape[1:], BF16),
            pltpu.VMEM((16, 8, width), BF16),
            pltpu.VMEM((16, 8, width), BF16),
            pltpu.SemaphoreType.DMA((60,)),
            pltpu.SemaphoreType.DMA((16, 4)),
            pltpu.SemaphoreType.DMA((8,)),
            pltpu.SemaphoreType.DMA((8,)),
            pltpu.SemaphoreType.DMA((16,)),
            pltpu.SemaphoreType.DMA((16,)),
        ],
        compiler_params=pltpu.CompilerParams(collective_id=0, has_side_effects=True),
        name="gather_project",
    )(lens, dest, wanted, tokens, norm_gains, wq, wkv, jnp.asarray(freq), ids, gates, pool, adapters)


def attend_kernel(lens, dest, group, q, k, v, pages, out, acc, turned, page_turned):
    ends = ends_of(lens)
    lane = lax.rem(lax.broadcasted_iota(I32, (1, 256), 1), 128)
    ones = jnp.ones((8, 128), BF16)

    def turn_step(b, carry):
        at = pl.ds(pl.multiple_of(b * 128, 128), 128)
        turned[0:HD, at] = v[at, :].astype(F32).T.astype(BF16)
        turned[HD : HD + 8, at] = ones
        return carry

    lax.fori_loop(0, v.shape[0] // 128, turn_step, 0)
    came = []
    for r in range(4):
        at = 0
        for g in range(8):
            at = at + g * (dest[g * 4 + r] == group[0] * 4 + r).astype(I32)
        came.append(at)
        page_turned[r, 0:HD] = pages[at, :, HD : 2 * HD].astype(F32).T.astype(BF16)
        page_turned[r, HD : HD + 8] = ones

    def block_step(block, carry):
        first = block * 128
        last = first + 127
        here = pl.ds(pl.multiple_of(first, 128), 128)
        queries = jnp.concatenate([q[here, 0:HD], q[here, HD : 2 * HD]], axis=0)
        rows = lane + first
        begin = start_of(rows, ends)
        low, high, low_start, high_start = 0, 0, 0, 0
        for end in ends[:3]:
            low = low + (first >= end).astype(I32)
            high = high + (last >= end).astype(I32)
            low_start = jnp.where(first >= end, end, low_start)
            high_start = jnp.where(last >= end, end, high_start)
        acc[...] = jnp.zeros_like(acc)

        def fold(top, keys, values, visible):
            scores = lax.dot_general(
                keys, queries, (((1,), (1,)), ((), ())), preferred_element_type=F32
            )
            if visible is not None:
                scores = jnp.where(visible, scores, -1e30)
            peak = jnp.maximum(top, jnp.max(scores, axis=0, keepdims=True))
            kept = jnp.exp2(top - peak)
            raised = jnp.exp2(scores - peak).astype(BF16)
            acc[...] = acc[...] * kept + jnp.dot(values, raised, preferred_element_type=F32)
            return peak

        def cached_step(r, top):
            begins = jnp.where(
                r == 0, 0, jnp.where(r == 1, ends[0], jnp.where(r == 2, ends[1], ends[2]))
            )
            page = jnp.where(
                r == 0, came[0], jnp.where(r == 1, came[1], jnp.where(r == 2, came[2], came[3]))
            )
            mine = jnp.broadcast_to(begin == begins, (CACHE, 256))
            return fold(top, pages[page, :, 0:HD], page_turned[r], mine)

        def masked_step(b, top):
            at = pl.ds(pl.multiple_of(b * 256, 256), 256)
            cols = lax.broadcasted_iota(I32, (256, 256), 0) + b * 256
            return fold(top, k[at, :], turned[:, at], (cols >= begin) & (cols <= rows))

        def plain_step(b, top):
            at = pl.ds(pl.multiple_of(b * 256, 256), 256)
            return fold(top, k[at, :], turned[:, at], None)

        top = jnp.full((1, 256), -1e30, F32)
        top = lax.fori_loop(low, high + 1, cached_step, top)
        start, stop = lax.div(low_start, 256), lax.div(last, 256)
        clear = jnp.minimum(jnp.maximum(lax.div(high_start + 255, 256), start), stop)
        top = lax.fori_loop(start, clear, masked_step, top)
        top = lax.fori_loop(clear, stop, plain_step, top)
        top = masked_step(stop, top)
        heads = acc[0:HD] / acc[HD : HD + 1]
        out[here, 0:HD] = heads[:, 0:128].T.astype(BF16)
        out[here, HD : 2 * HD] = heads[:, 128:256].T.astype(BF16)
        return carry

    lax.fori_loop(0, q.shape[0] // 128, block_step, 0)


def attend(q, k, v, pages, lens, dest, group):
    rows = q.shape[0]
    smem = pl.BlockSpec(memory_space=pltpu.SMEM)
    vmem = pl.BlockSpec(memory_space=pltpu.VMEM)
    return pl.pallas_call(
        attend_kernel,
        out_shape=jax.ShapeDtypeStruct((rows, 2 * HD), BF16),
        in_specs=[smem] * 3 + [vmem] * 4,
        out_specs=vmem,
        scratch_shapes=[
            pltpu.VMEM((HD + 8, 256), F32),
            pltpu.VMEM((HD + 8, rows), BF16),
            pltpu.VMEM((4, HD + 8, CACHE), BF16),
        ],
        name="attend_heads",
    )(lens, dest, group, q, k, v, pages)


ORDER = (2, 1, 3, 0)


def reduce_kernel(
    heads, choice, w, tok, gain, hidden, hnorm, far, near, own, rx_far, rx_near, far2, near2, rx_far2, rx_near2,
    ssem, far_sem, near_sem, far2_sem, near2_sem,
):
    me, y, z = place()
    barrier = meet_neighbours(y, z)
    link = Sender(y, z, ssem)

    def partial(half, first):
        one = lax.rem(y * (1 - half) + z * half + first, SIDE)
        parts = []
        for offset in ORDER:
            two = lax.rem(z * (1 - half) + y * half + offset, SIDE)
            s = one * (4 - 3 * half) + two * (1 + 3 * half)
            parts.append(pl.ds(pl.multiple_of(s * 128 + half * 64, 64), 64))
        rows = jnp.concatenate([heads[at, :] for at in parts], axis=0).astype(F32)
        named = jnp.concatenate([choice[at, :] for at in parts], axis=0)
        gated = [rows[:, j * HD : (j + 1) * HD] * named[:, 2 + j : 3 + j] for j in (0, 1)]
        mixed = []
        for e in range(AEXP):
            both = [jnp.where(named[:, j : j + 1] == float(e), gated[j], 0.0) for j in (0, 1)]
            mixed.append((both[0] + both[1]).astype(BF16))
        return jnp.dot(jnp.concatenate(mixed, axis=1), w[...], preferred_element_type=F32)

    def far_step(half, carry):
        far[half] = partial(half, 2).astype(BF16).reshape(far.shape[1:])
        return carry

    lax.fori_loop(0, 2, far_step, 0)
    pl.semaphore_wait(barrier, 4)
    for i in range(4):
        for half in (0, 1):
            for p in (0, 1):
                link.send(
                    far.at[half, i, p], rx_far.at[half, p, i], far_sem.at[half, p, i], half, 1 + 2 * p
                )

    def near_step(n, carry):
        half, way = lax.div(n, 2), lax.rem(n, 2)
        near[half, way] = partial(half, 1 + 2 * way).astype(BF16).reshape(near.shape[2:])
        return carry

    lax.fori_loop(0, 4, near_step, 0)

    def send_near(half, way, i, p):
        link.send(
            near.at[half, way, i, p],
            rx_near.at[half, way, i, p],
            near_sem.at[half, way, i, p],
            half,
            1 + 2 * way,
        )

    for i in range(4):
        for half in (0, 1):
            for way in (0, 1):
                send_near(half, way, i, 1 - way)

    def own_step(half, carry):
        own[half] = partial(half, 0).reshape(own.shape[1:])
        return carry

    lax.fori_loop(0, 2, own_step, 0)

    for i in range(4):
        for half in (0, 1):
            for way in (0, 1):
                link.arrive(rx_far.at[half, way, i], far_sem.at[half, way, i])
                near[half, way, i, way] = (
                    near[half, way, i, way].astype(F32) + rx_far[half, way, i].astype(F32)
                ).astype(BF16)
        for half in (0, 1):
            for way in (0, 1):
                send_near(half, way, i, way)

    def total(half, i):
        for way in (0, 1):
            for p in (0, 1):
                link.arrive(rx_near.at[half, way, i, p], near_sem.at[half, way, i, p])
        summed = own[half, i]
        for way in (0, 1):
            summed = summed + rx_near[half, way, i].astype(F32)
        return summed

    def send_near2(half, way, p):
        link.send(
            near2.at[half, way, p],
            rx_near2.at[half, way, p],
            near2_sem.at[half, way, p],
            1 - half,
            1 + 2 * way,
        )

    for half in (0, 1):
        far2[half] = total(half, 0).astype(BF16)
    for half in (0, 1):
        for p in (0, 1):
            link.send(far2.at[half, p], rx_far2.at[half, p], far2_sem.at[half, p], 1 - half, 1 + 2 * p)
    for way in (0, 1):
        for half in (0, 1):
            near2[half, way] = total(half, 1 + way).astype(BF16)
        for half in (0, 1):
            send_near2(half, way, 1 - way)
    for way in (0, 1):
        for half in (0, 1):
            link.arrive(rx_far2.at[half, way], far2_sem.at[half, way])
            near2[half, way, way] = (
                near2[half, way, way].astype(F32) + rx_far2[half, way].astype(F32)
            ).astype(BF16)
        for half in (0, 1):
            send_near2(half, way, way)
    for half in (0, 1):
        own[half, 3] = total(half, 3)
    for half in (0, 1):
        summed = own[half, 3]
        for way in (0, 1):
            for p in (0, 1):
                link.arrive(rx_near2.at[half, way, p], near2_sem.at[half, way, p])
            summed = summed + rx_near2[half, way].astype(F32)
        rows = slice(half * 64, (half + 1) * 64)
        state = (tok[rows, :].astype(F32) + summed.reshape(64, -1)).astype(BF16)
        hidden[rows, :] = state
        hnorm[rows, :] = rms_scale(state, gain[1:2])
    link.finish()


def reduce_out(heads, choice, w_out, tokens, norm_gains):
    width = tokens.shape[1]
    vmem = pl.BlockSpec(memory_space=pltpu.VMEM)
    shape = jax.ShapeDtypeStruct(tokens.shape, BF16)
    piece = (32, width)
    dma = pltpu.SemaphoreType.DMA
    return pl.pallas_call(
        reduce_kernel,
        out_shape=(shape, shape),
        in_specs=[vmem] * 5,
        out_specs=(vmem, vmem),
        scratch_shapes=[
            pltpu.VMEM((2, 4, 2) + piece, BF16),
            pltpu.VMEM((2, 2, 4, 2) + piece, BF16),
            pltpu.VMEM((2, 4, 2) + piece, F32),
            pltpu.VMEM((2, 2, 4) + piece, BF16),
            pltpu.VMEM((2, 2, 4, 2) + piece, BF16),
            pltpu.VMEM((2, 2) + piece, BF16),
            pltpu.VMEM((2, 2, 2) + piece, BF16),
            pltpu.VMEM((2, 2) + piece, BF16),
            pltpu.VMEM((2, 2, 2) + piece, BF16),
            dma((60,)),
            dma((2, 2, 4)),
            dma((2, 2, 4, 2)),
            dma((2, 2)),
            dma((2, 2, 2)),
        ],
        compiler_params=pltpu.CompilerParams(collective_id=1, has_side_effects=True),
        name="project_reduce",
    )(heads, choice, w_out, tokens, norm_gains)


def expert_kernel(
    lens, hidden, hnorm, w_in, w_down, ids, gates, factors, out,
    packed, rx, back, ret, raw, w, wd, both, placed, table,
    wsem, dsem, ssem, rsem, bsem, esem, fsem, gsem,
):
    me = lax.axis_index("exp")
    width = hidden.shape[1]
    hidden_units = w_down.shape[0]
    barrier = meet_all("exp", me, 16)
    down = pltpu.make_async_copy(w_down, wd, dsem)
    down.start()

    def fetch(c):
        return pltpu.make_async_copy(
            w_in.at[pl.ds(c * 256, 256)], raw.at[lax.rem(c, 2)], wsem.at[lax.rem(c, 2)]
        )

    fetch(0).start()
    expert = lax.broadcasted_iota(I32, (8, 128), 0)
    hits = [ids[j : j + 1, :] == expert for j in (0, 1)]
    hit = (hits[0] | hits[1]).astype(F32)
    gate = jnp.where(hits[0], gates[0:1, :], 0.0) + jnp.where(hits[1], gates[1:2, :], 0.0)
    before = lax.broadcasted_iota(I32, (128, 128), 0) < lax.broadcasted_iota(I32, (128, 128), 1)
    rank = jnp.dot(hit.astype(BF16), before.astype(BF16), preferred_element_type=F32)
    slot = lax.broadcasted_iota(I32, (CAP, 128), 0).astype(F32)
    for e in range(EXPERTS):
        placed[e] = jnp.where((rank[e : e + 1] == slot) & (hit[e : e + 1] > 0.0), 1.0, 0.0)
    choice = placed[...].reshape(EXPERTS * CAP, 128).astype(BF16)
    packed[...] = (
        jnp.dot(choice, hnorm[...], preferred_element_type=F32).astype(BF16).reshape(packed.shape)
    )
    pl.semaphore_wait(barrier, 15)
    copies = []
    for step in range(1, 16):
        other = lax.rem(me + step, 16)
        copy = to_peer(
            "exp", other, packed.at[lax.div(other, 2)], rx.at[step], ssem.at[step], rsem.at[step]
        )
        copy.start()
        copies.append(copy)
    rx[0] = packed[lax.div(me, 2)]

    rows256 = lax.broadcasted_iota(I32, (256, 256), 0)
    cols256 = lax.broadcasted_iota(I32, (256, 256), 1)
    by2 = (cols256 == lax.rem(rows256, 128) * 2 + lax.div(rows256, 128)).astype(BF16)

    def split_step(c, carry):
        @pl.when(c + 1 < 8)
        def _():
            fetch(c + 1).start()

        fetch(c).wait()
        for b in (0, 1):
            rows = raw[lax.rem(c, 2), b * 128 : (b + 1) * 128].reshape(256, hidden_units)
            part = jnp.dot(by2, rows, preferred_element_type=F32).astype(BF16)
            at = pl.ds(pl.multiple_of(c * 256 + b * 128, 128), 128)
            w[at, 0:hidden_units] = part[0:128]
            w[at, hidden_units : 2 * hidden_units] = part[128:256]
        return carry

    lax.fori_loop(0, 8, split_step, 0)
    down.wait()
    shares = []
    for part in (0, 1):
        for step in range(8 * part, 8 * part + 8):
            if step:
                copies[step - 1].wait_recv()
        if part == 1:
            for step in range(1, 16):
                copy = to_peer(
                    "exp", lax.rem(me + step, 16), factors, table.at[me], fsem.at[step], gsem.at[step]
                )
                copy.start()
                shares.append(copy)
        rows = rx[8 * part : 8 * part + 8].reshape(8 * CAP, width)
        both[...] = jnp.dot(rows, w[...], preferred_element_type=F32)
        gated = both[:, 0:hidden_units]
        inner = (gated / (1.0 + jnp.exp(-gated)) * both[:, hidden_units : 2 * hidden_units]).astype(BF16)
        back[8 * part : 8 * part + 8] = (
            jnp.dot(inner, wd[...], preferred_element_type=F32).astype(BF16).reshape(8, CAP, width)
        )
        for step in range(8 * part, 8 * part + 8):
            if step:
                copy = to_peer(
                    "exp", lax.rem(me + 16 - step, 16), back.at[step], ret.at[me],
                    bsem.at[step], esem.at[step],
                )
                copy.start()
                copies.append(copy)
            else:
                ret[me] = back[0]
    table[me] = factors[...]
    for copy in shares:
        copy.wait()
    rows = table[...].reshape(16 * 8, width)
    lowrank = lax.dot_general(
        hnorm[...], rows, (((1,), (1,)), ((), ())), preferred_element_type=F32
    )
    tokens = lax.broadcasted_iota(I32, (128, 1), 0) + me * 128
    ends = ends_of(lens)
    segment = jnp.zeros_like(tokens)
    for end in ends[:3]:
        segment = segment + (tokens >= end).astype(I32)
    lane = lax.broadcasted_iota(I32, (128, 128), 1)
    mine = (lax.div(lane, 32) == segment) & (lax.rem(lane, 32) < 16)
    lowrank = pltpu.roll(jnp.where(mine, lowrank, 0.0), 16, 1).astype(BF16)
    delta = jnp.dot(lowrank, rows, preferred_element_type=F32)
    total = hidden[...].astype(F32) + delta
    for step in range(1, 16):
        copies[14 + step].wait_recv()
    weight = jnp.concatenate(
        [placed[e // 2] * gate[e // 2 : e // 2 + 1] for e in range(16)], axis=0
    )
    high = weight.astype(BF16)
    low = (weight - high.astype(F32)).astype(BF16)
    came = ret[...].reshape(16 * CAP, width)
    for factor in (high, low):
        total = total + lax.dot_general(
            factor, came, (((0,), (0,)), ((), ())), preferred_element_type=F32
        )
    out[...] = total.astype(BF16)
    for copy in copies:
        copy.wait_send()


def experts(hidden, hnorm, w_in, w_down, ids, gates, factors, lens):
    rows, width = hidden.shape
    units = w_down.shape[0]
    smem = pl.BlockSpec(memory_space=pltpu.SMEM)
    vmem = pl.BlockSpec(memory_space=pltpu.VMEM)
    hbm = pl.BlockSpec(memory_space=pl.ANY)
    dma = pltpu.SemaphoreType.DMA
    return pl.pallas_call(
        expert_kernel,
        out_shape=jax.ShapeDtypeStruct((rows, width), BF16),
        in_specs=[smem, vmem, vmem, hbm, hbm, vmem, vmem, vmem],
        out_specs=vmem,
        scratch_shapes=[
            pltpu.VMEM((EXPERTS, CAP, width), BF16),
            pltpu.VMEM((16, CAP, width), BF16),
            pltpu.VMEM((16, CAP, width), BF16),
            pltpu.VMEM((16, CAP, width), BF16),
            pltpu.VMEM((2, 256, 2, units), BF16),
            pltpu.VMEM((width, 2 * units), BF16),
            pltpu.VMEM((units, width), BF16),
            pltpu.VMEM((8 * CAP, 2 * units), F32),
            pltpu.VMEM((EXPERTS, CAP, 128), F32),
            pltpu.VMEM((16, 8, width), BF16),
            dma((2,)),
            dma,
            dma((16,)),
            dma((16,)),
            dma((16,)),
            dma((16,)),
            dma((16,)),
            dma((16,)),
        ],
        compiler_params=pltpu.CompilerParams(collective_id=2, has_side_effects=True),
        name="expert_exchange",
    )(lens, hidden, hnorm, w_in, w_down, ids, gates, factors)


def on_device(
    tokens,
    norm_gains,
    w_query,
    w_keyval,
    w_out,
    page_pool,
    page_dest,
    prompt_lens,
    att_ids,
    att_gates,
    w_in,
    w_down,
    moe_ids,
    moe_gates,
    adapters,
    req_adapter,
):
    width = tokens.shape[1]
    lens = prompt_lens.reshape(-1)
    group = lax.axis_index("req").reshape(1)
    q, k, v, pages, factors, choice = project(
        tokens,
        norm_gains,
        w_query.reshape(width * AEXP, HD),
        w_keyval.reshape(width * 2, HD),
        lens,
        att_ids.T,
        att_gates.T,
        page_dest,
        req_adapter,
        page_pool.reshape(page_pool.shape[0], CACHE, 2 * HD),
        adapters.reshape(adapters.shape[0], 4, 8, width),
    )
    heads = attend(q, k, v, pages, lens, page_dest, group)
    hidden, hnorm = reduce_out(heads, choice, w_out.reshape(-1, width), tokens, norm_gains)
    return experts(
        hidden,
        hnorm,
        w_in,
        w_down,
        moe_ids.T,
        moe_gates.T,
        factors,
        lens,
    )


def solution(mesh):
    in_specs = (
        P(("req", "exp"), None),
        P(),
        P(None, None, "exp"),
        P(None, None, "exp"),
        P(None, "exp", None),
        P("req", None, "exp", None),
        P(),
        P("req", None),
        P("req", None),
        P("req", None),
        P(None, None, "exp"),
        P("exp", None),
        P(("req", "exp"), None),
        P(("req", "exp"), None),
        P("exp", None, None, None),
        P(),
    )
    out_specs = P(("req", "exp"), None)
    return jax.shard_map(
        on_device, mesh=mesh, in_specs=in_specs, out_specs=out_specs, check_vma=False
    )
```
